256 devices in a mesh: dp: 2 (over z_lo), node: 16 (over x, z_hi), local: 8 (over y, core).
Axes of the slice: x: 4, y: 4, z: 8 (z_hi: 4, z_lo: 2; z = z_hi * 2 + z_lo), core: 2. Of those that a mesh axis runs over, the one named last changes fastest.
Arguments:
- tokens_in: bfloat16 [2, 16, 64, 16, 3584], P('dp', 'node'), may hold values from -6 to 6
- grad_rows: bfloat16 [2, 16, 64, 16, 3584], P('dp', 'node'), may hold values from -6 to 6
- combine_weights: float32 [2, 16, 64, 16], P('dp', 'node'), may hold values from 0.05 to 1
- live_counts: int32 [2, 16, 16], P('dp', 'node'), may hold values from 0 to 64, as said below
- w_gate: bfloat16 [16, 3584, 2048], P('node', None, 'local'), may hold values from -0.09375 to 0.09375
- w_up: bfloat16 [16, 3584, 2048], P('node', None, 'local'), may hold values from -0.09375 to 0.09375
- w_down: bfloat16 [16, 3584, 2048], P('node', None, 'local'), may hold values from -0.125 to 0.125
Outputs:
- d_tokens: bfloat16 [2, 16, 64, 16, 3584], P('dp', 'node', 'local')
- grad_gate: bfloat16 [16, 3584, 2048], P('node', 'dp', 'local')
- grad_up: bfloat16 [16, 3584, 2048], P('node', 'dp', 'local')
- grad_down: bfloat16 [16, 3584, 2048], P('node', 'dp', 'local')
The draws below stay inside these ranges and needn't reach their ends.
Inputs may be any that keep to these rules, and one draw needn't show every extreme that they name: `live_counts`: each replica has some source and expert pair with all 64 slots live; loads differ strongly between experts.
All inputs are finite; a program needn't handle non-finite values.
Results may differ from the reference program's by a relative error of at most 0.019.
Values may be sent and summed in bfloat16 or wider, within the bound.
A program may use at most 128 MiB of HBM per device.

```python
import math
import jax
import jax.numpy as jnp
from jax import lax

D = 3584
HID = 2048
SLOTS = 64
REPLICAS = 2
NODES = 16


def draw_live_counts(key, part):
    key_hot = jax.random.fold_in(key, 11)
    key_base = jax.random.fold_in(key, 12)
    key_pick = jax.random.fold_in(key, 13)
    hotness = jax.random.randint(key_hot, (REPLICAS, NODES, 1), 1, 5)
    base_load = jax.random.randint(key_base, (REPLICAS, NODES, NODES), 0, SLOTS // 3 + 2)
    loads = jnp.minimum(base_load * hotness, SLOTS).reshape(REPLICAS, NODES * NODES)
    picked = jax.random.randint(key_pick, (REPLICAS,), 0, NODES * NODES)
    chosen = jnp.arange(NODES * NODES, dtype=jnp.int32)[None, :] == picked[:, None]
    loads = jnp.where(chosen, SLOTS, loads)
    return loads.reshape(REPLICAS, NODES, NODES).astype(jnp.int32)


def levels(stream_key, shape, cuts, low, high):
    loudness = 1.0
    for axis_at, shards_of in cuts:
        draws = jax.random.uniform(jax.random.fold_in(jax.random.fold_in(stream_key, 6), axis_at), (shards_of,), jnp.float32, low / len(cuts), high / len(cuts))
        loudness = loudness * jnp.repeat(jnp.exp(draws), shape[axis_at] // shards_of).reshape((-1,) + (1,) * (len(shape) - 1 - axis_at))
    return loudness


def gaussian(stream_key, dims, width, limit, split=(), kind=jnp.bfloat16):
    drawn = width * jax.random.normal(stream_key, dims, jnp.float32)
    if split:
        drawn = drawn * levels(stream_key, dims, split, -0.22, 0.18)
    return jnp.clip(drawn, -limit, limit).astype(kind)


def setup_inputs(seed: int = 0) -> dict:
    splits = jax.random.split(jax.random.key(seed), 8)
    return {
        "tokens_in": gaussian(splits[0], (REPLICAS, NODES, SLOTS, NODES, D), 1.0, 6.0, ((0, 2), (1, 16))),
        "grad_rows": gaussian(splits[1], (REPLICAS, NODES, SLOTS, NODES, D), 1.0, 6.0, ((0, 2), (1, 16))),
        "combine_weights": jnp.clip(jnp.exp(math.log(1.0) - 2.9957323 * jax.random.uniform(splits[2], (REPLICAS, NODES, SLOTS, NODES), jnp.float32) ** levels(splits[2], (REPLICAS, NODES, SLOTS, NODES), ((0, 2), (1, 16)), -0.2, 0.2)), 0.05, 1.0),
        "live_counts": draw_live_counts(jax.random.fold_in(splits[7], 71), 0),
        "w_gate": gaussian(splits[4], (NODES, D, HID), D ** -0.5, 0.09375, ((0, 16), (2, 8))),
        "w_up": gaussian(splits[5], (NODES, D, HID), D ** -0.5, 0.09375, ((0, 16), (2, 8))),
        "w_down": gaussian(splits[6], (NODES, D, HID), HID ** -0.5, 0.125, ((0, 16), (2, 8))),
    }


def expert_pass(token_block, grad_block, weight_block, count_row, gate_weight, up_weight, down_weight):
    live_mask = (jnp.arange(SLOTS, dtype=jnp.int32)[:, None] < count_row[None, :]).astype(jnp.float32)
    scaled_rows = (grad_block.astype(jnp.float32) * (weight_block * live_mask)[:, :, None]).astype(jnp.bfloat16)
    scaled_rows = scaled_rows.reshape(SLOTS * NODES, D)
    flat_tokens = token_block.reshape(SLOTS * NODES, D)
    gate_pre = jnp.dot(flat_tokens, gate_weight, preferred_element_type=jnp.float32)
    up_pre = jnp.dot(flat_tokens, up_weight, preferred_element_type=jnp.float32)
    sigmoid_gate = jax.nn.sigmoid(gate_pre)
    activated = gate_pre * sigmoid_gate
    hidden = (activated * up_pre).astype(jnp.bfloat16)
    hidden_grad = jnp.dot(scaled_rows, down_weight, preferred_element_type=jnp.float32)
    gate_grad = (hidden_grad * up_pre * sigmoid_gate * (1.0 + gate_pre * (1.0 - sigmoid_gate))).astype(jnp.bfloat16)
    up_grad = (hidden_grad * activated).astype(jnp.bfloat16)
    input_grad = jnp.dot(gate_grad, gate_weight.T, preferred_element_type=jnp.float32) + jnp.dot(up_grad, up_weight.T, preferred_element_type=jnp.float32)
    gate_part = jnp.dot(flat_tokens.T, gate_grad, preferred_element_type=jnp.float32).astype(jnp.bfloat16)
    up_part = jnp.dot(flat_tokens.T, up_grad, preferred_element_type=jnp.float32).astype(jnp.bfloat16)
    down_part = jnp.dot(scaled_rows.T, hidden, preferred_element_type=jnp.float32).astype(jnp.bfloat16)
    return input_grad.astype(jnp.bfloat16).reshape(SLOTS, NODES, D), gate_part, up_part, down_part


def reference(tokens_in, grad_rows, combine_weights, live_counts, w_gate, w_up, w_down):
    def per_expert(expert):
        gate_weight = w_gate[expert]
        up_weight = w_up[expert]
        down_weight = w_down[expert]
        inputs_list = []
        gate_total = jnp.zeros((D, HID), jnp.float32)
        up_total = jnp.zeros((D, HID), jnp.float32)
        down_total = jnp.zeros((D, HID), jnp.float32)
        for replica in range(REPLICAS):
            input_grad, gate_part, up_part, down_part = expert_pass(
                tokens_in[replica, expert], grad_rows[replica, expert], combine_weights[replica, expert],
                live_counts[replica, expert], gate_weight, up_weight, down_weight)
            inputs_list.append(input_grad)
            gate_total = gate_total + lax.optimization_barrier(gate_part).astype(jnp.float32)
            up_total = up_total + lax.optimization_barrier(up_part).astype(jnp.float32)
            down_total = down_total + lax.optimization_barrier(down_part).astype(jnp.float32)
        return (jnp.stack(inputs_list), gate_total.astype(jnp.bfloat16), up_total.astype(jnp.bfloat16), down_total.astype(jnp.bfloat16))

    stacked, grad_gate, grad_up, grad_down = lax.map(per_expert, jnp.arange(NODES, dtype=jnp.int32))
    d_tokens = jnp.transpose(stacked, (1, 3, 2, 0, 4))
    return d_tokens, grad_gate, grad_up, grad_down
```

```python
import jax
import jax.numpy as jnp
from jax import lax
from jax.sharding import PartitionSpec as P

SWAP = [(0, 1), (1, 0)]


def on_device(tokens_in, grad_rows, combine_weights, live_counts, w_gate, w_up, w_down):
    slot_count = tokens_in.shape[2]
    node_count = tokens_in.shape[3]
    feature_width = tokens_in.shape[4]
    row_count = slot_count * node_count
    half = feature_width // 2
    gate_weight = w_gate[0]
    up_weight = w_up[0]
    down_weight = w_down[0]
    mine = lax.axis_index("dp")
    live_mask = (
        lax.broadcasted_iota(jnp.int32, (slot_count, node_count), 0) < live_counts[0, 0][None, :]
    ).astype(jnp.float32)
    scaled_rows = (
        grad_rows[0, 0].astype(jnp.float32) * (combine_weights[0, 0] * live_mask)[:, :, None]
    ).astype(jnp.bfloat16)
    scaled_rows = scaled_rows.reshape(row_count, feature_width)
    flat_tokens = tokens_in[0, 0].reshape(row_count, feature_width)
    gate_pre = jnp.dot(flat_tokens, gate_weight, preferred_element_type=jnp.float32)
    up_pre = jnp.dot(flat_tokens, up_weight, preferred_element_type=jnp.float32)
    sigmoid_gate = jax.nn.sigmoid(gate_pre)
    activated = gate_pre * sigmoid_gate
    hidden = (activated * up_pre).astype(jnp.bfloat16)
    hidden_grad = jnp.dot(scaled_rows, down_weight, preferred_element_type=jnp.float32)
    gate_grad = (
        hidden_grad * up_pre * sigmoid_gate * (1.0 + gate_pre * (1.0 - sigmoid_gate))
    ).astype(jnp.bfloat16)
    up_grad = (hidden_grad * activated).astype(jnp.bfloat16)

    def weight_grad(rows, grads):
        full = lax.dot_general(
            rows, grads, (((0,), (0,)), ((), ())), preferred_element_type=jnp.float32
        ).astype(jnp.bfloat16)
        keep = lax.dynamic_slice_in_dim(full, mine * half, half, 0)
        send = lax.dynamic_slice_in_dim(full, (1 - mine) * half, half, 0)
        return keep, lax.ppermute(send, "dp", SWAP)

    down_keep, down_got = weight_grad(scaled_rows, hidden)
    gate_keep, gate_got = weight_grad(flat_tokens, gate_grad)
    up_keep, up_got = weight_grad(flat_tokens, up_grad)

    total = lax.dot_general(
        gate_grad, gate_weight, (((1,), (1,)), ((), ())), preferred_element_type=jnp.float32
    )
    total = total + lax.dot_general(
        up_grad, up_weight, (((1,), (1,)), ((), ())), preferred_element_type=jnp.float32
    )
    summed = lax.psum_scatter(
        total.astype(jnp.bfloat16), "local", scatter_dimension=0, tiled=True
    )
    summed = lax.optimization_barrier(summed)
    summed = summed.reshape(-1, node_count, feature_width)
    returned = lax.all_to_all(summed, "node", split_axis=1, concat_axis=1, tiled=True)
    d_tokens = returned[None, None]

    def join(keep, got):
        return (keep.astype(jnp.float32) + got.astype(jnp.float32)).astype(jnp.bfloat16)[None]

    return (
        d_tokens,
        join(gate_keep, gate_got),
        join(up_keep, up_got),
        join(down_keep, down_got),
    )


def solution(mesh):
    return jax.shard_map(
        on_device,
        mesh=mesh,
        in_specs=(
            P("dp", "node", None, None, None),
            P("dp", "node", None, None, None),
            P("dp", "node", None, None),
            P("dp", "node", None),
            P("node", None, "local"),
            P("node", None, "local"),
            P("node", None, "local"),
        ),
        out_specs=(
            P("dp", "node", "local", None, None),
            P("node", "dp", "local"),
            P("node", "dp", "local"),
            P("node", "dp", "local"),
        ),
        check_vma=False,
    )
```

```python
import functools

import jax
import jax.numpy as jnp
from jax import lax
from jax.experimental import pallas as pl
from jax.experimental.pallas import tpu as pltpu
from jax.sharding import PartitionSpec as P

RING = 4
BF16 = jnp.bfloat16
F32 = jnp.float32


def dot_nt(a, b):
    return lax.dot_general(a, b, (((1,), (1,)), ((), ())), preferred_element_type=F32)


def dot_tn(a, b):
    return lax.dot_general(a, b, (((0,), (0,)), ((), ())), preferred_element_type=F32)


def swap_matrix(size, inner_in, inner_out):
    row = lax.broadcasted_iota(jnp.int32, (size, size), 0)
    col = lax.broadcasted_iota(jnp.int32, (size, size), 1)
    source = (row % inner_out) * inner_in + row // inner_out
    return (col == source).astype(BF16)


def layer_kernel(
    nodes, chunk, tile,
    tok_hbm, grd_hbm, scale_ref, wg_hbm, wu_hbm, wd_hbm,
    dtok_out, gate_out, up_out, down_out,
    tok, scl, wg, wu, wd, hid, act, actp, tok_o, act_o,
    msend, mrecv, csum, orecv, nrecv, afin, arecv, dfin, dsend, drecv, wfin,
    load_sem, tz_sem, az_sem, m_sem, ag_sem, fw_sem, o_sem, n_sem, a_sem, dz_sem, out_sem,
):
    rows, width = tok.shape
    hl = wg.shape[1]
    half = width // 2
    group = rows // (2 * RING)
    block = rows // RING
    slots = group // nodes
    steps = width // chunk
    side = chunk // 2
    tiles = half // tile

    mine = lax.axis_index("dp")
    node = lax.axis_index("node")
    local = lax.axis_index("local")
    core = lax.rem(local, 2)
    place = lax.div(local, 2)
    other = 1 - mine
    mate = local + 1 - 2 * core

    def at_place(step):
        return lax.rem(place + step, RING)

    def peer(step):
        return at_place(step) * 2 + core

    def load(src, dst, index):
        return pltpu.make_async_copy(src, dst, load_sem.at[index])

    def block_rows(b):
        return pl.ds(pl.multiple_of(b * block, block), block)

    def tok_load(b):
        return load(tok_hbm.at[block_rows(b)], tok.at[block_rows(b)], 3 + b)

    def grd_load(b):
        return load(grd_hbm.at[block_rows(b)], scl.at[block_rows(b)], 3 + RING + b)

    load_wg = load(wg_hbm, wg, 0)
    load_wu = load(wu_hbm, wu, 1)
    load_wd = load(wd_hbm, wd, 2)
    load_wg.start()
    tok_load(0).start()
    load_wu.start()
    load_wd.start()
    grd_load(0).start()
    for b in range(1, RING):
        tok_load(b).start()
        grd_load(b).start()

    barrier = pltpu.get_barrier_semaphore()
    pl.semaphore_signal(barrier, inc=1, device_id={"dp": other})
    pl.semaphore_signal(barrier, inc=1, device_id={"local": mate})
    for step in range(1, RING):
        pl.semaphore_signal(barrier, inc=1, device_id={"local": peer(step)})

    def greet(i, carry):
        pl.semaphore_signal(barrier, inc=1, device_id={"node": lax.rem(node + i, nodes)})
        return carry

    lax.fori_loop(1, nodes, greet, 0)
    pl.semaphore_wait(barrier, 2 + RING - 1 + nodes - 1)

    def group_rows(l):
        return pl.ds(pl.multiple_of(l * group, group), group)

    tz = pltpu.make_async_remote_copy(
        tok_hbm.at[group_rows(local), pl.ds(pl.multiple_of(other * half, 128), half)],
        tok_o.at[group_rows(local)],
        tz_sem.at[0], tz_sem.at[1], device_id={"dp": other},
    )
    tz.start()

    def az(b):
        return pltpu.make_async_remote_copy(
            act.at[block_rows(b)], act_o.at[block_rows(b)],
            az_sem.at[0, b], az_sem.at[1, b], device_id={"dp": other},
        )

    swap_in = swap_matrix(group, nodes, slots)
    load_wg.wait()
    load_wu.wait()
    load_wd.wait()

    def forward(b, carry):
        here = block_rows(b)
        tok_load(b).wait()
        rows_in = tok[here, :]
        gate = jnp.dot(rows_in, wg[...], preferred_element_type=F32)
        up = jnp.dot(rows_in, wu[...], preferred_element_type=F32)
        grd_load(b).wait()
        scaled = (scl[here, :].astype(F32) * scale_ref[here, :]).astype(BF16)
        scl[here, :] = scaled
        back = jnp.dot(scaled, wd[...], preferred_element_type=F32)
        sig = jax.nn.sigmoid(gate)
        silu = gate * sig
        hid[here, :] = (silu * up).astype(BF16)
        gate_grad = (back * up * sig * (1.0 + gate * (1.0 - sig))).astype(BF16)
        up_grad = (back * silu).astype(BF16)
        act[here, :hl] = gate_grad
        act[here, hl:] = up_grad
        az(b).start()
        for i in range(2):
            part = slice(i * group, (i + 1) * group)
            there = pl.ds(pl.multiple_of((i * RING + b) * group, group), group)
            actp[there, :hl] = jnp.dot(
                swap_in, gate_grad[part], preferred_element_type=F32
            ).astype(BF16)
            actp[there, hl:] = jnp.dot(
                swap_in, up_grad[part], preferred_element_type=F32
            ).astype(BF16)
        return carry

    lax.fori_loop(0, RING, forward, 0)

    def partial(which, q):
        cols = pl.ds(pl.multiple_of(q * chunk, chunk), chunk)
        here = pl.ds(pl.multiple_of(which * (rows // 2), rows // 2), rows // 2)
        return dot_nt(actp[here, :hl], wg[cols, :]) + dot_nt(actp[here, hl:], wu[cols, :])

    def to_mate(q):
        return pltpu.make_async_remote_copy(
            msend.at[q], mrecv.at[q], m_sem.at[0, q], m_sem.at[1, q], device_id={"local": mate}
        )

    def give(q, carry):
        msend[q] = partial(1 - core, q).astype(BF16)
        to_mate(q).start()
        return carry

    lax.fori_loop(0, steps, give, 0)

    def spread(step):
        return pltpu.make_async_remote_copy(
            tok_o.at[group_rows(local)], tok_o.at[group_rows(local)],
            ag_sem.at[0, step], ag_sem.at[1, step], device_id={"local": peer(step)},
        )

    def hand_on(step):
        rows_of = group_rows(peer(step))
        return pltpu.make_async_remote_copy(
            tok_o.at[rows_of], tok_o.at[rows_of],
            fw_sem.at[0, step], fw_sem.at[1, step], device_id={"local": mate},
        )

    tz.wait_recv()
    for step in range(1, RING):
        spread(step).start()
    hand_on(0).start()

    def part_rows(step):
        return pl.ds(pl.multiple_of(at_place(step) * group, group), group)

    def opposite(q, way):
        return pltpu.make_async_remote_copy(
            csum.at[q, part_rows(2), pl.ds(way * side, side)],
            orecv.at[q, way],
            o_sem.at[0, q, way], o_sem.at[1, q, way],
            device_id={"local": peer(1 if way == 0 else RING - 1)},
        )

    def neighbour(q, way):
        step = 1 if way == 0 else RING - 1
        return pltpu.make_async_remote_copy(
            csum.at[q, part_rows(step)],
            nrecv.at[q, way],
            n_sem.at[0, q, way], n_sem.at[1, q, way],
            device_id={"local": peer(step)},
        )

    def to_nodes(q):
        return pltpu.make_async_remote_copy(
            afin.at[q, pl.ds(0, nodes - 1)], arecv.at[q, pl.ds(0, nodes - 1)],
            a_sem.at[0, q], a_sem.at[1, q], device_id={"node": lax.rem(node + 1, nodes)},
        )

    def chip_sum(q):
        to_mate(q).wait_recv()
        total = partial(core, q) + mrecv[q].astype(F32)
        csum[q] = total.astype(BF16)
        opposite(q, 0).start()
        opposite(q, 1).start()

    def pass_on(q):
        for way in range(2):
            opposite(q, way).wait_recv()
            here = part_rows(1 if way == 0 else RING - 1)
            cols = slice(way * side, (way + 1) * side)
            csum[q, here, cols] = (
                csum[q, here, cols].astype(F32) + orecv[q, way].astype(F32)
            ).astype(BF16)
            neighbour(q, way).start()

    def finish(q):
        neighbour(q, 0).wait_recv()
        neighbour(q, 1).wait_recv()
        total = csum[q, part_rows(0)].astype(F32) + nrecv[q, 0].astype(F32) + nrecv[q, 1].astype(F32)
        afin[q] = total.reshape(nodes, slots, chunk).astype(BF16)
        arecv[q, node] = afin[q, node]

        def send(i, carry):
            to = lax.rem(node + i, nodes)
            pltpu.make_async_remote_copy(
                afin.at[q, to], arecv.at[q, node],
                a_sem.at[0, q], a_sem.at[1, q], device_id={"node": to},
            ).start()
            return carry

        lax.fori_loop(1, nodes, send, 0)

    def tile_cols(which, k):
        return pl.ds(pl.multiple_of(which * half + k * tile, 128), tile)

    def tile_rows(k):
        return pl.ds(pl.multiple_of(k * tile, tile), tile)

    def dz(k):
        return pltpu.make_async_remote_copy(
            dsend.at[tile_rows(k)], drecv.at[tile_rows(k)],
            dz_sem.at[0, k], dz_sem.at[1, k], device_id={"dp": other},
        )

    def down_other(k, carry):
        dsend[tile_rows(k), :] = dot_tn(scl[:, tile_cols(other, k)], hid[...]).astype(BF16)
        dz(k).start()
        return carry

    chip_sum(0)
    chip_sum(1)
    lax.fori_loop(0, tiles, down_other, 0)

    def pipeline(s, carry):
        @pl.when(s < steps)
        def _():
            chip_sum(s)

        @pl.when(jnp.logical_and(s >= 1, s < steps + 1))
        def _():
            pass_on(s - 1)

        @pl.when(s >= 3)
        def _():
            finish(s - 3)

        return carry

    pass_on(0)
    lax.fori_loop(2, steps + 3, pipeline, 0)

    for step in range(1, RING):
        pltpu.make_async_remote_copy(
            tok_o.at[group_rows(peer(RING - step))], tok_o.at[group_rows(peer(RING - step))],
            ag_sem.at[0, step], ag_sem.at[1, step], device_id={"local": peer(step)},
        ).wait_recv()
        hand_on(RING - step).start()
    for step in range(RING):
        hand_on(step).wait_recv()
    for b in range(RING):
        az(b).wait_recv()

    def put(which, k, out):
        return pltpu.make_async_copy(
            wfin.at[which, tile_rows(k)], out.at[tile_rows(k)], out_sem.at[which, k]
        )

    def weights(k, carry):
        here = tile_rows(k)
        dz(k).wait_recv()
        down = dot_tn(scl[:, tile_cols(mine, k)], hid[...]).astype(BF16).astype(F32)
        wfin[2, here, :] = (down + drecv[here, :].astype(F32)).astype(BF16)
        put(2, k, down_out).start()
        both = dot_tn(tok[:, tile_cols(mine, k)], act[...]) + dot_tn(
            tok_o[:, tile_cols(0, k)], act_o[...]
        )
        wfin[0, here, :] = both[:, :hl].astype(BF16)
        wfin[1, here, :] = both[:, hl:].astype(BF16)
        put(0, k, gate_out).start()
        put(1, k, up_out).start()
        return carry

    lax.fori_loop(0, tiles, weights, 0)

    swap_out = swap_matrix(group, slots, nodes)

    def put_rows(q):
        cols = pl.ds(pl.multiple_of(q * chunk, chunk), chunk)
        return pltpu.make_async_copy(dfin.at[q], dtok_out.at[:, cols], out_sem.at[3, q])

    def collect(q, carry):
        to_nodes(q).wait_recv()
        got = arecv[q].astype(F32).reshape(group, chunk).astype(BF16)
        dfin[q] = jnp.dot(swap_out, got, preferred_element_type=F32).astype(BF16)
        put_rows(q).start()
        return carry

    lax.fori_loop(0, steps, collect, 0)

    tz.wait_send()
    for b in range(RING):
        az(b).wait_send()
    for step in range(1, RING):
        spread(step).wait_send()
    for step in range(RING):
        hand_on(step).wait_send()

    def drain(q, carry):
        to_mate(q).wait_send()
        for way in range(2):
            opposite(q, way).wait_send()
            neighbour(q, way).wait_send()
        to_nodes(q).wait_send()
        put_rows(q).wait()
        return carry

    lax.fori_loop(0, steps, drain, 0)

    def drain_weights(k, carry):
        dz(k).wait_send()
        put(0, k, gate_out).wait()
        put(1, k, up_out).wait()
        put(2, k, down_out).wait()
        return carry

    lax.fori_loop(0, tiles, drain_weights, 0)


def on_device(chunk, tile, tokens_in, grad_rows, combine_weights, live_counts, w_gate, w_up, w_down):
    slot_count, nodes, width = tokens_in.shape[2:]
    rows = slot_count * nodes
    hl = w_gate.shape[2]
    half = width // 2
    group = rows // (2 * RING)
    steps = width // chunk
    tiles = half // tile
    live_mask = (
        lax.broadcasted_iota(jnp.int32, (slot_count, nodes), 0) < live_counts[0, 0][None, :]
    ).astype(F32)
    scale = (combine_weights[0, 0] * live_mask).reshape(rows, 1)
    anywhere = pl.BlockSpec(memory_space=pl.ANY)
    dma = pltpu.SemaphoreType.DMA
    vmem = pltpu.VMEM
    weight_shape = jax.ShapeDtypeStruct((half, hl), BF16)
    d_tokens, gate, up, down = pl.pallas_call(
        functools.partial(layer_kernel, nodes, chunk, tile),
        out_shape=(jax.ShapeDtypeStruct((group, width), BF16), weight_shape, weight_shape, weight_shape),
        in_specs=[anywhere, anywhere, pl.BlockSpec(memory_space=vmem), anywhere, anywhere, anywhere],
        out_specs=(anywhere, anywhere, anywhere, anywhere),
        scratch_shapes=[
            vmem((rows, width), BF16),
            vmem((rows, width), BF16),
            vmem((width, hl), BF16),
            vmem((width, hl), BF16),
            vmem((width, hl), BF16),
            vmem((rows, hl), BF16),
            vmem((rows, 2 * hl), BF16),
            vmem((rows, 2 * hl), BF16),
            vmem((rows, half), BF16),
            vmem((rows, 2 * hl), BF16),
            vmem((steps, rows // 2, chunk), BF16),
            vmem((steps, rows // 2, chunk), BF16),
            vmem((steps, rows // 2, chunk), BF16),
            vmem((steps, 2, group, chunk // 2), BF16),
            vmem((steps, 2, group, chunk), BF16),
            vmem((steps, nodes, group // nodes, chunk), BF16),
            vmem((steps, nodes, group // nodes, chunk), BF16),
            vmem((steps, group, chunk), BF16),
            vmem((half, hl), BF16),
            vmem((half, hl), BF16),
            vmem((3, half, hl), BF16),
            dma((3 + 2 * RING,)),
            dma((2,)),
            dma((2, RING)),
            dma((2, steps)),
            dma((2, RING)),
            dma((2, RING)),
            dma((2, steps, 2)),
            dma((2, steps, 2)),
            dma((2, steps)),
            dma((2, tiles)),
            dma((4, max(tiles, steps))),
        ],
        compiler_params=pltpu.CompilerParams(
            collective_id=0, has_side_effects=True, vmem_limit_bytes=VMEM_LIMIT
        ),
        name="expert_backward",
    )(
        tokens_in[0, 0].reshape(rows, width),
        grad_rows[0, 0].reshape(rows, width),
        scale,
        w_gate[0],
        w_up[0],
        w_down[0],
    )
    return (
        d_tokens.reshape(1, 1, group // nodes, nodes, width),
        gate[None],
        up[None],
        down[None],
    )


VMEM_LIMIT = 62 * 1024 * 1024
CHUNK = 512
TILE = 256


def solution(mesh):
    return jax.shard_map(
        functools.partial(on_device, CHUNK, TILE),
        mesh=mesh,
        in_specs=(
            P("dp", "node", None, None, None),
            P("dp", "node", None, None, None),
            P("dp", "node", None, None),
            P("dp", "node", None),
            P("node", None, "local"),
            P("node", None, "local"),
            P("node", None, "local"),
        ),
        out_specs=(
            P("dp", "node", "local", None, None),
            P("node", "dp", "local"),
            P("node", "dp", "local"),
            P("node", "dp", "local"),
        ),
        check_vma=False,
    )
```

```python
import functools

import jax
import jax.numpy as jnp
from jax import lax
from jax.experimental import pallas as pl
from jax.experimental.pallas import tpu as pltpu
from jax.sharding import PartitionSpec as P

RING = 4
BF16 = jnp.bfloat16
F32 = jnp.float32


def dot_nt(a, b):
    return lax.dot_general(a, b, (((1,), (1,)), ((), ())), preferred_element_type=F32)


def dot_tn(a, b):
    return lax.dot_general(a, b, (((0,), (0,)), ((), ())), preferred_element_type=F32)


def swap_matrix(size, inner_in, inner_out):
    row = lax.broadcasted_iota(jnp.int32, (size, size), 0)
    col = lax.broadcasted_iota(jnp.int32, (size, size), 1)
    source = (row % inner_out) * inner_in + row // inner_out
    return (col == source).astype(BF16)


def layer_kernel(
    nodes, chunk, tile,
    tok_hbm, grd_hbm, weight_ref, count_ref, wg_hbm, wu_hbm, wd_hbm,
    dtok_out, gate_out, up_out, down_out,
    tok, scl, wg, wu, wd, hid, act, actp, tok_o, act_o,
    msend, mrecv, csum, orecv, nrecv, afin, arecv, dfin, dsend, drecv, wfin,
    load_sem, tz_sem, az_sem, m_sem, ag_sem, fw_sem, o_sem, n_sem, a_sem, dz_sem, out_sem,
):
    rows, width = tok.shape
    hl = wg.shape[1]
    half = width // 2
    group = rows // (2 * RING)
    block = rows // RING
    slots = group // nodes
    piece = group // RING
    steps = width // chunk
    side = chunk // 2
    tiles = half // tile

    mine = lax.axis_index("dp")
    node = lax.axis_index("node")
    local = lax.axis_index("local")
    core = lax.rem(local, 2)
    place = lax.div(local, 2)
    other = 1 - mine
    mate = local + 1 - 2 * core

    def at_place(step):
        return lax.rem(place + step, RING)

    def peer(step):
        return at_place(step) * 2 + core

    def load(src, dst, index):
        return pltpu.make_async_copy(src, dst, load_sem.at[index])

    def block_rows(b):
        return pl.ds(pl.multiple_of(b * block, block), block)

    def tok_load(b):
        return load(tok_hbm.at[block_rows(b)], tok.at[block_rows(b)], 3 + b)

    def grd_load(b):
        return load(grd_hbm.at[block_rows(b)], scl.at[block_rows(b)], 3 + RING + b)

    load_wg = load(wg_hbm, wg, 0)
    load_wu = load(wu_hbm, wu, 1)
    load_wd = load(wd_hbm, wd, 2)
    load_wg.start()
    load_wu.start()
    tok_load(0).start()
    load_wd.start()
    grd_load(0).start()

    barrier = pltpu.get_barrier_semaphore()
    pl.semaphore_signal(barrier, inc=1, device_id={"dp": other})
    pl.semaphore_signal(barrier, inc=1, device_id={"local": mate})
    for step in range(1, RING):
        pl.semaphore_signal(barrier, inc=1, device_id={"local": peer(step)})

    def greet(i, carry):
        pl.semaphore_signal(barrier, inc=1, device_id={"node": lax.rem(node + i, nodes)})
        return carry

    lax.fori_loop(1, nodes, greet, 0)
    pl.semaphore_wait(barrier, 2 + RING - 1 + nodes - 1)

    def group_rows(l):
        return pl.ds(pl.multiple_of(l * group, group), group)

    def piece_rows(l, p):
        return pl.ds(pl.multiple_of(l * group + p * piece, piece), piece)

    def tz(p):
        return pltpu.make_async_remote_copy(
            tok_hbm.at[piece_rows(local, p), pl.ds(pl.multiple_of(other * half, 128), half)],
            tok_o.at[piece_rows(local, p)],
            tz_sem.at[0, p], tz_sem.at[1, p], device_id={"dp": other},
        )

    for p in range(RING):
        tz(p).start()
    tok_load(1).start()
    grd_load(1).start()

    def spread(step, p):
        return pltpu.make_async_remote_copy(
            tok_o.at[piece_rows(local, p)], tok_o.at[piece_rows(local, p)],
            ag_sem.at[0, step, p], ag_sem.at[1, step, p], device_id={"local": peer(step)},
        )

    def spread_piece(p):
        tz(p).wait_recv()
        for step in range(1, RING):
            spread(step, p).start()

    def az(b):
        return pltpu.make_async_remote_copy(
            act.at[block_rows(b)], act_o.at[block_rows(b)],
            az_sem.at[0, b], az_sem.at[1, b], device_id={"dp": other},
        )

    swap_in = swap_matrix(group, nodes, slots)

    eye = lax.broadcasted_iota(jnp.int32, (nodes, nodes), 0) == lax.broadcasted_iota(
        jnp.int32, (nodes, nodes), 1
    )
    counts = jnp.broadcast_to(count_ref[...].astype(F32), (nodes, nodes))
    counts = jnp.sum(jnp.where(eye, counts, 0.0), axis=1, keepdims=True)
    slot_total = weight_ref.shape[1]
    slot_at = lax.broadcasted_iota(jnp.int32, (nodes, slot_total), 1).astype(F32)
    live_weights = jnp.where(slot_at < counts, weight_ref[...], 0.0)
    row_weights = jnp.tile(live_weights, (block // nodes, 1))
    row_slot = lax.broadcasted_iota(jnp.int32, (block, slot_total), 0) // nodes
    slot_lane = lax.broadcasted_iota(jnp.int32, (block, slot_total), 1)

    load_wg.wait()
    load_wu.wait()

    def forward(b, carry):
        here = block_rows(b)
        tok_load(b).wait()
        grd_load(b).wait()

        @pl.when(b == 0)
        def _():
            load_wd.wait()

        @pl.when(b < RING - 2)
        def _():
            tok_load(b + 2).start()
            grd_load(b + 2).start()

        scale = jnp.sum(
            jnp.where(slot_lane == row_slot + b * (block // nodes), row_weights, 0.0),
            axis=1, keepdims=True,
        )
        rows_in = tok[here, :]
        gate = jnp.dot(rows_in, wg[...], preferred_element_type=F32)
        up = jnp.dot(rows_in, wu[...], preferred_element_type=F32)
        scaled = (scl[here, :].astype(F32) * scale).astype(BF16)
        scl[here, :] = scaled
        back = jnp.dot(scaled, wd[...], preferred_element_type=F32)
        sig = jax.nn.sigmoid(gate)
        silu = gate * sig
        hid[here, :] = (silu * up).astype(BF16)
        gate_grad = (back * up * sig * (1.0 + gate * (1.0 - sig))).astype(BF16)
        up_grad = (back * silu).astype(BF16)
        act[here, :hl] = gate_grad
        act[here, hl:] = up_grad
        az(b).start()
        for i in range(2):
            part = slice(i * group, (i + 1) * group)
            there = pl.ds(pl.multiple_of((i * RING + b) * group, group), group)
            actp[there, :hl] = jnp.dot(
                swap_in, gate_grad[part], preferred_element_type=F32
            ).astype(BF16)
            actp[there, hl:] = jnp.dot(
                swap_in, up_grad[part], preferred_element_type=F32
            ).astype(BF16)

        @pl.when(b >= 1)
        def _():
            spread_piece(b - 1)

        return carry

    lax.fori_loop(0, RING, forward, 0)

    def partial(which, q):
        cols = pl.ds(pl.multiple_of(q * chunk, chunk), chunk)
        here = pl.ds(pl.multiple_of(which * (rows // 2), rows // 2), rows // 2)
        return dot_nt(actp[here, :hl], wg[cols, :]) + dot_nt(actp[here, hl:], wu[cols, :])

    def to_mate(q):
        return pltpu.make_async_remote_copy(
            msend.at[q], mrecv.at[q], m_sem.at[0, q], m_sem.at[1, q], device_id={"local": mate}
        )

    def give(q):
        msend[q] = partial(1 - core, q).astype(BF16)
        to_mate(q).start()

    def hand_on(step):
        rows_of = group_rows(peer(step))
        return pltpu.make_async_remote_copy(
            tok_o.at[rows_of], tok_o.at[rows_of],
            fw_sem.at[0, step], fw_sem.at[1, step], device_id={"local": mate},
        )

    def part_rows(step):
        return pl.ds(pl.multiple_of(at_place(step) * group, group), group)

    def opposite(q, way):
        return pltpu.make_async_remote_copy(
            csum.at[q, part_rows(2), pl.ds(way * side, side)],
            orecv.at[q, way],
            o_sem.at[0, q, way], o_sem.at[1, q, way],
            device_id={"local": peer(1 if way == 0 else RING - 1)},
        )

    def neighbour(q, way):
        step = 1 if way == 0 else RING - 1
        return pltpu.make_async_remote_copy(
            csum.at[q, part_rows(step)],
            nrecv.at[q, way],
            n_sem.at[0, q, way], n_sem.at[1, q, way],
            device_id={"local": peer(step)},
        )

    def to_nodes(q):
        return pltpu.make_async_remote_copy(
            afin.at[q, pl.ds(0, nodes - 1)], arecv.at[q, pl.ds(0, nodes - 1)],
            a_sem.at[0, q], a_sem.at[1, q], device_id={"node": lax.rem(node + 1, nodes)},
        )

    def chip_sum(q):
        to_mate(q).wait_recv()
        total = partial(core, q) + mrecv[q].astype(F32)
        csum[q] = total.astype(BF16)
        opposite(q, 0).start()
        opposite(q, 1).start()

    def pass_on(q):
        for way in range(2):
            opposite(q, way).wait_recv()
            here = part_rows(1 if way == 0 else RING - 1)
            cols = slice(way * side, (way + 1) * side)
            csum[q, here, cols] = (
                csum[q, here, cols].astype(F32) + orecv[q, way].astype(F32)
            ).astype(BF16)
            neighbour(q, way).start()

    def finish(q):
        neighbour(q, 0).wait_recv()
        neighbour(q, 1).wait_recv()
        total = csum[q, part_rows(0)].astype(F32) + nrecv[q, 0].astype(F32) + nrecv[q, 1].astype(F32)
        afin[q] = total.reshape(nodes, slots, chunk).astype(BF16)
        arecv[q, node] = afin[q, node]

        def send(i, carry):
            to = lax.rem(node + i, nodes)
            pltpu.make_async_remote_copy(
                afin.at[q, to], arecv.at[q, node],
                a_sem.at[0, q], a_sem.at[1, q], device_id={"node": to},
            ).start()
            return carry

        lax.fori_loop(1, nodes, send, 0)

    def tile_cols(which, k):
        return pl.ds(pl.multiple_of(which * half + k * tile, 128), tile)

    def tile_rows(k):
        return pl.ds(pl.multiple_of(k * tile, tile), tile)

    def dz(k):
        return pltpu.make_async_remote_copy(
            dsend.at[tile_rows(k)], drecv.at[tile_rows(k)],
            dz_sem.at[0, k], dz_sem.at[1, k], device_id={"dp": other},
        )

    def down_other(k):
        dsend[tile_rows(k), :] = dot_tn(scl[:, tile_cols(other, k)], hid[...]).astype(BF16)
        dz(k).start()

    def pipeline(s, carry):
        @pl.when(s < steps)
        def _():
            give(s)

        @pl.when(s == 1)
        def _():
            spread_piece(RING - 1)
            hand_on(0).start()

        @pl.when(jnp.logical_and(s >= 2, s < steps + 2))
        def _():
            chip_sum(s - 2)

        for i in range(2):
            k = (s - 2) * 2 + i

            @pl.when(jnp.logical_and(k >= 0, k < tiles))
            def _():
                down_other(k)

        @pl.when(jnp.logical_and(s >= 4, s < steps + 4))
        def _():
            pass_on(s - 4)

        @pl.when(s == 6)
        def _():
            hand_on_arrivals()

        @pl.when(s >= 6)
        def _():
            finish(s - 6)

        return carry

    def hand_on_arrivals():
        for step in range(1, RING):
            for p in range(RING):
                rows_of = piece_rows(peer(RING - step), p)
                pltpu.make_async_remote_copy(
                    tok_o.at[rows_of], tok_o.at[rows_of],
                    ag_sem.at[0, step, p], ag_sem.at[1, step, p], device_id={"local": peer(step)},
                ).wait_recv()
            hand_on(RING - step).start()

    lax.fori_loop(0, steps + 6, pipeline, 0)

    for step in range(RING):
        hand_on(step).wait_recv()
    for b in range(RING):
        az(b).wait_recv()

    def put(which, k, out):
        return pltpu.make_async_copy(
            wfin.at[which, tile_rows(k)], out.at[tile_rows(k)], out_sem.at[which, k]
        )

    def weights(k, carry):
        here = tile_rows(k)
        dz(k).wait_recv()
        down = dot_tn(scl[:, tile_cols(mine, k)], hid[...]).astype(BF16).astype(F32)
        wfin[2, here, :] = (down + drecv[here, :].astype(F32)).astype(BF16)
        put(2, k, down_out).start()
        both = dot_tn(tok[:, tile_cols(mine, k)], act[...]) + dot_tn(
            tok_o[:, tile_cols(0, k)], act_o[...]
        )
        wfin[0, here, :] = both[:, :hl].astype(BF16)
        wfin[1, here, :] = both[:, hl:].astype(BF16)
        put(0, k, gate_out).start()
        put(1, k, up_out).start()
        return carry

    lax.fori_loop(0, tiles, weights, 0)

    swap_out = swap_matrix(group, slots, nodes)

    def put_rows(q):
        cols = pl.ds(pl.multiple_of(q * chunk, chunk), chunk)
        return pltpu.make_async_copy(dfin.at[q], dtok_out.at[:, cols], out_sem.at[3, q])

    def collect(q, carry):
        to_nodes(q).wait_recv()
        got = arecv[q].astype(F32).reshape(group, chunk).astype(BF16)
        dfin[q] = jnp.dot(swap_out, got, preferred_element_type=F32).astype(BF16)
        put_rows(q).start()
        return carry

    lax.fori_loop(0, steps, collect, 0)

    for b in range(RING):
        tz(b).wait_send()
        az(b).wait_send()
    for step in range(1, RING):
        for p in range(RING):
            spread(step, p).wait_send()
    for step in range(RING):
        hand_on(step).wait_send()

    def drain(q, carry):
        to_mate(q).wait_send()
        for way in range(2):
            opposite(q, way).wait_send()
            neighbour(q, way).wait_send()
        to_nodes(q).wait_send()
        put_rows(q).wait()
        return carry

    lax.fori_loop(0, steps, drain, 0)

    def drain_weights(k, carry):
        dz(k).wait_send()
        put(0, k, gate_out).wait()
        put(1, k, up_out).wait()
        put(2, k, down_out).wait()
        return carry

    lax.fori_loop(0, tiles, drain_weights, 0)


def copy_kernel(count, *refs):
    sems = refs[2 * count]
    copies = []
    for i in range(count):
        src, dst = refs[i], refs[count + i]
        part = src.shape[0] // 2
        for h in range(2):
            span = pl.ds(h * part, part)
            copies.append(pltpu.make_async_copy(src.at[span], dst.at[span], sems.at[2 * i + h]))
    for copy in copies:
        copy.start()
    for copy in copies:
        copy.wait()


def on_device(chunk, tile, tokens_in, grad_rows, combine_weights, live_counts, w_gate, w_up, w_down):
    slot_count, nodes, width = tokens_in.shape[2:]
    rows = slot_count * nodes
    hl = w_gate.shape[2]
    half = width // 2
    group = rows // (2 * RING)
    steps = width // chunk
    tiles = half // tile
    anywhere = pl.BlockSpec(memory_space=pl.ANY)
    dma = pltpu.SemaphoreType.DMA
    vmem = pltpu.VMEM
    weight_shape = jax.ShapeDtypeStruct((half, hl), BF16)
    held = pl.pallas_call(
        functools.partial(layer_kernel, nodes, chunk, tile),
        out_shape=(jax.ShapeDtypeStruct((group, width), BF16), weight_shape, weight_shape, weight_shape),
        in_specs=[anywhere, anywhere, pl.BlockSpec(memory_space=vmem),
                  pl.BlockSpec(memory_space=vmem), anywhere, anywhere, anywhere],
        out_specs=(anywhere, anywhere, anywhere, anywhere),
        scratch_shapes=[
            vmem((rows, width), BF16),
            vmem((rows, width), BF16),
            vmem((width, hl), BF16),
            vmem((width, hl), BF16),
            vmem((width, hl), BF16),
            vmem((rows, hl), BF16),
            vmem((rows, 2 * hl), BF16),
            vmem((rows, 2 * hl), BF16),
            vmem((rows, half), BF16),
            vmem((rows, 2 * hl), BF16),
            vmem((steps, rows // 2, chunk), BF16),
            vmem((steps, rows // 2, chunk), BF16),
            vmem((steps, rows // 2, chunk), BF16),
            vmem((steps, 2, group, chunk // 2), BF16),
            vmem((steps, 2, group, chunk), BF16),
            vmem((steps, nodes, group // nodes, chunk), BF16),
            vmem((steps, nodes, group // nodes, chunk), BF16),
            vmem((steps, group, chunk), BF16),
            vmem((half, hl), BF16),
            vmem((half, hl), BF16),
            vmem((3, half, hl), BF16),
            dma((3 + 2 * RING,)),
            dma((2, RING)),
            dma((2, RING)),
            dma((2, steps)),
            dma((2, RING, RING)),
            dma((2, RING)),
            dma((2, steps, 2)),
            dma((2, steps, 2)),
            dma((2, steps)),
            dma((2, tiles)),
            dma((4, max(tiles, steps))),
        ],
        compiler_params=pltpu.CompilerParams(
            collective_id=0, has_side_effects=True, vmem_limit_bytes=VMEM_LIMIT
        ),
        name="expert_backward",
    )(
        tokens_in[0, 0].reshape(rows, width),
        grad_rows[0, 0].reshape(rows, width),
        combine_weights[0, 0].T,
        live_counts[0],
        w_gate[0],
        w_up[0],
        w_down[0],
    )
    d_tokens, gate, up, down = pl.pallas_call(
        functools.partial(copy_kernel, len(held)),
        out_shape=tuple(jax.ShapeDtypeStruct(a.shape, a.dtype) for a in held),
        in_specs=[anywhere] * len(held),
        out_specs=tuple([anywhere] * len(held)),
        scratch_shapes=[dma((2 * len(held),))],
        name="write_out",
    )(*held)
    return (
        d_tokens.reshape(1, 1, group // nodes, nodes, width),
        gate[None],
        up[None],
        down[None],
    )


VMEM_LIMIT = 62 * 1024 * 1024
CHUNK = 512
TILE = 256


def solution(mesh):
    return jax.shard_map(
        functools.partial(on_device, CHUNK, TILE),
        mesh=mesh,
        in_specs=(
            P("dp", "node", None, None, None),
            P("dp", "node", None, None, None),
            P("dp", "node", None, None),
            P("dp", "node", None),
            P("node", None, "local"),
            P("node", None, "local"),
            P("node", None, "local"),
        ),
        out_specs=(
            P("dp", "node", "local", None, None),
            P("node", "dp", "local"),
            P("node", "dp", "local"),
            P("node", "dp", "local"),
        ),
        check_vma=False,
    )
```

```python
import functools

import jax
import jax.numpy as jnp
from jax import lax
from jax.experimental import pallas as pl
from jax.experimental.pallas import tpu as pltpu
from jax.sharding import PartitionSpec as P

RING = 4
BF16 = jnp.bfloat16
F32 = jnp.float32


def dot_nt(a, b):
    return lax.dot_general(a, b, (((1,), (1,)), ((), ())), preferred_element_type=F32)


def dot_tn(a, b):
    return lax.dot_general(a, b, (((0,), (0,)), ((), ())), preferred_element_type=F32)


def swap_matrix(size, inner_in, inner_out):
    row = lax.broadcasted_iota(jnp.int32, (size, size), 0)
    col = lax.broadcasted_iota(jnp.int32, (size, size), 1)
    source = (row % inner_out) * inner_in + row // inner_out
    return (col == source).astype(BF16)


def layer_kernel(
    nodes, chunk, tile,
    tok_hbm, grd_hbm, weight_ref, count_ref, wg_hbm, wu_hbm, wd_hbm,
    dtok_out, gate_out, up_out, down_out,
    tok, scl, wg, wu, wd, hid, act, actp, tok_o, act_o,
    msend, mrecv, csum, orecv, nrecv, afin, arecv, dfin, dsend, drecv, wfin,
    load_sem, tz_sem, az_sem, m_sem, ag_sem, fw_sem, o_sem, n_sem, a_sem, dz_sem, out_sem,
):
    rows, width = tok.shape
    hl = wg.shape[1]
    half = width // 2
    group = rows // (2 * RING)
    block = rows // RING
    slots = group // nodes
    piece = group // RING
    steps = width // chunk
    side = chunk // 2
    tiles = half // tile

    mine = lax.axis_index("dp")
    node = lax.axis_index("node")
    local = lax.axis_index("local")
    core = lax.rem(local, 2)
    place = lax.div(local, 2)
    other = 1 - mine
    mate = local + 1 - 2 * core

    def at_place(step):
        return lax.rem(place + step, RING)

    def peer(step):
        return at_place(step) * 2 + core

    def load(src, dst, index):
        return pltpu.make_async_copy(src, dst, load_sem.at[index])

    def block_rows(b):
        return pl.ds(pl.multiple_of(b * block, block), block)

    def tok_load(b):
        return load(tok_hbm.at[block_rows(b)], tok.at[block_rows(b)], 3 + b)

    def grd_load(b):
        return load(grd_hbm.at[block_rows(b)], scl.at[block_rows(b)], 3 + RING + b)

    load_wg = load(wg_hbm, wg, 0)
    load_wu = load(wu_hbm, wu, 1)
    load_wd = load(wd_hbm, wd, 2)
    load_wg.start()
    load_wu.start()
    tok_load(0).start()
    load_wd.start()
    grd_load(0).start()

    barrier = pltpu.get_barrier_semaphore()
    pl.semaphore_signal(barrier, inc=1, device_id={"dp": other})
    pl.semaphore_signal(barrier, inc=1, device_id={"local": mate})
    for step in range(1, RING):
        pl.semaphore_signal(barrier, inc=1, device_id={"local": peer(step)})

    def greet(i, carry):
        pl.semaphore_signal(barrier, inc=1, device_id={"node": lax.rem(node + i, nodes)})
        return carry

    lax.fori_loop(1, nodes, greet, 0)
    pl.semaphore_wait(barrier, 2 + RING - 1 + nodes - 1)

    def group_rows(l):
        return pl.ds(pl.multiple_of(l * group, group), group)

    def piece_rows(l, p):
        return pl.ds(pl.multiple_of(l * group + p * piece, piece), piece)

    def tz(p):
        return pltpu.make_async_remote_copy(
            tok_hbm.at[piece_rows(local, p), pl.ds(pl.multiple_of(other * half, 128), half)],
            tok_o.at[piece_rows(local, p)],
            tz_sem.at[0, p], tz_sem.at[1, p], device_id={"dp": other},
        )

    for p in range(RING):
        tz(p).start()
    tok_load(1).start()
    grd_load(1).start()

    def spread(step, p):
        return pltpu.make_async_remote_copy(
            tok_o.at[piece_rows(local, p)], tok_o.at[piece_rows(local, p)],
            ag_sem.at[0, step, p], ag_sem.at[1, step, p], device_id={"local": peer(step)},
        )

    def spread_piece(p):
        tz(p).wait_recv()
        for step in range(1, RING):
            spread(step, p).start()

    def az(b):
        return pltpu.make_async_remote_copy(
            act.at[block_rows(b)], act_o.at[block_rows(b)],
            az_sem.at[0, b], az_sem.at[1, b], device_id={"dp": other},
        )

    swap_in = swap_matrix(group, nodes, slots)

    eye = lax.broadcasted_iota(jnp.int32, (nodes, nodes), 0) == lax.broadcasted_iota(
        jnp.int32, (nodes, nodes), 1
    )
    counts = jnp.broadcast_to(count_ref[...].astype(F32), (nodes, nodes))
    counts = jnp.sum(jnp.where(eye, counts, 0.0), axis=1, keepdims=True)
    slot_total = weight_ref.shape[1]
    slot_at = lax.broadcasted_iota(jnp.int32, (nodes, slot_total), 1).astype(F32)
    live_weights = jnp.where(slot_at < counts, weight_ref[...], 0.0)
    row_weights = jnp.tile(live_weights, (block // nodes, 1))
    row_slot = lax.broadcasted_iota(jnp.int32, (block, slot_total), 0) // nodes
    slot_lane = lax.broadcasted_iota(jnp.int32, (block, slot_total), 1)

    load_wg.wait()
    load_wu.wait()

    def forward(b, carry):
        here = block_rows(b)
        tok_load(b).wait()
        grd_load(b).wait()

        @pl.when(b == 0)
        def _():
            load_wd.wait()

        @pl.when(b < RING - 2)
        def _():
            tok_load(b + 2).start()
            grd_load(b + 2).start()

        scale = jnp.sum(
            jnp.where(slot_lane == row_slot + b * (block // nodes), row_weights, 0.0),
            axis=1, keepdims=True,
        )
        rows_in = tok[here, :]
        gate = jnp.dot(rows_in, wg[...], preferred_element_type=F32)
        up = jnp.dot(rows_in, wu[...], preferred_element_type=F32)
        scaled = (scl[here, :].astype(F32) * scale).astype(BF16)
        scl[here, :] = scaled
        back = jnp.dot(scaled, wd[...], preferred_element_type=F32)
        sig = jax.nn.sigmoid(gate)
        silu = gate * sig
        hid[here, :] = (silu * up).astype(BF16)
        gate_grad = (back * up * sig * (1.0 + gate * (1.0 - sig))).astype(BF16)
        up_grad = (back * silu).astype(BF16)
        act[here, :hl] = gate_grad
        act[here, hl:] = up_grad
        az(b).start()
        for i in range(2):
            part = slice(i * group, (i + 1) * group)
            there = pl.ds(pl.multiple_of((i * RING + b) * group, group), group)
            actp[there, :hl] = jnp.dot(
                swap_in, gate_grad[part], preferred_element_type=F32
            ).astype(BF16)
            actp[there, hl:] = jnp.dot(
                swap_in, up_grad[part], preferred_element_type=F32
            ).astype(BF16)

        @pl.when(b >= 1)
        def _():
            spread_piece(b - 1)

        return carry

    lax.fori_loop(0, RING, forward, 0)

    def partial(which, q):
        cols = pl.ds(pl.multiple_of(q * chunk, chunk), chunk)
        here = pl.ds(pl.multiple_of(which * (rows // 2), rows // 2), rows // 2)
        return dot_nt(actp[here, :hl], wg[cols, :]) + dot_nt(actp[here, hl:], wu[cols, :])

    def to_mate(q):
        return pltpu.make_async_remote_copy(
            msend.at[q], mrecv.at[q], m_sem.at[0, q], m_sem.at[1, q], device_id={"local": mate}
        )

    def give(q):
        msend[q] = partial(1 - core, q).astype(BF16)
        to_mate(q).start()

    def hand_on(step):
        rows_of = group_rows(peer(step))
        return pltpu.make_async_remote_copy(
            tok_o.at[rows_of], tok_o.at[rows_of],
            fw_sem.at[0, step], fw_sem.at[1, step], device_id={"local": mate},
        )

    def part_rows(step):
        return pl.ds(pl.multiple_of(at_place(step) * group, group), group)

    def opposite(q, way):
        return pltpu.make_async_remote_copy(
            csum.at[q, part_rows(2), pl.ds(way * side, side)],
            orecv.at[q, way],
            o_sem.at[0, q, way], o_sem.at[1, q, way],
            device_id={"local": peer(1 if way == 0 else RING - 1)},
        )

    def neighbour(q, way):
        step = 1 if way == 0 else RING - 1
        return pltpu.make_async_remote_copy(
            csum.at[q, part_rows(step)],
            nrecv.at[q, way],
            n_sem.at[0, q, way], n_sem.at[1, q, way],
            device_id={"local": peer(step)},
        )

    def to_nodes(q):
        return pltpu.make_async_remote_copy(
            afin.at[q, pl.ds(0, nodes - 1)], arecv.at[q, pl.ds(0, nodes - 1)],
            a_sem.at[0, q], a_sem.at[1, q], device_id={"node": lax.rem(node + 1, nodes)},
        )

    def chip_sum(q):
        to_mate(q).wait_recv()
        total = partial(core, q) + mrecv[q].astype(F32)
        csum[q] = total.astype(BF16)
        opposite(q, 0).start()
        opposite(q, 1).start()

    def pass_on(q):
        for way in range(2):
            opposite(q, way).wait_recv()
            here = part_rows(1 if way == 0 else RING - 1)
            cols = slice(way * side, (way + 1) * side)
            csum[q, here, cols] = (
                csum[q, here, cols].astype(F32) + orecv[q, way].astype(F32)
            ).astype(BF16)
            neighbour(q, way).start()

    def finish(q):
        neighbour(q, 0).wait_recv()
        neighbour(q, 1).wait_recv()
        total = csum[q, part_rows(0)].astype(F32) + nrecv[q, 0].astype(F32) + nrecv[q, 1].astype(F32)
        afin[q] = total.reshape(nodes, slots, chunk).astype(BF16)
        arecv[q, node] = afin[q, node]

        def send(i, carry):
            to = lax.rem(node + i, nodes)
            pltpu.make_async_remote_copy(
                afin.at[q, to], arecv.at[q, node],
                a_sem.at[0, q], a_sem.at[1, q], device_id={"node": to},
            ).start()
            return carry

        lax.fori_loop(1, nodes, send, 0)

    def tile_cols(which, k):
        return pl.ds(pl.multiple_of(which * half + k * tile, 128), tile)

    def tile_rows(k):
        return pl.ds(pl.multiple_of(k * tile, tile), tile)

    def dz(k):
        return pltpu.make_async_remote_copy(
            dsend.at[tile_rows(k)], drecv.at[tile_rows(k)],
            dz_sem.at[0, k], dz_sem.at[1, k], device_id={"dp": other},
        )

    def down_other(k):
        dsend[tile_rows(k), :] = dot_tn(scl[:, tile_cols(other, k)], hid[...]).astype(BF16)
        dz(k).start()

    def pipeline(s, carry):
        @pl.when(s < steps)
        def _():
            give(s)

        @pl.when(s == 1)
        def _():
            spread_piece(RING - 1)
            hand_on(0).start()

        @pl.when(jnp.logical_and(s >= 2, s < steps + 2))
        def _():
            chip_sum(s - 2)

        for i in range(2):
            k = (s - 2) * 2 + i

            @pl.when(jnp.logical_and(k >= 0, k < tiles))
            def _():
                down_other(k)

        @pl.when(jnp.logical_and(s >= 4, s < steps + 4))
        def _():
            pass_on(s - 4)

        @pl.when(s == 6)
        def _():
            hand_on_arrivals()

        @pl.when(s >= 6)
        def _():
            finish(s - 6)

        return carry

    def hand_on_arrivals():
        for step in range(1, RING):
            for p in range(RING):
                rows_of = piece_rows(peer(RING - step), p)
                pltpu.make_async_remote_copy(
                    tok_o.at[rows_of], tok_o.at[rows_of],
                    ag_sem.at[0, step, p], ag_sem.at[1, step, p], device_id={"local": peer(step)},
                ).wait_recv()
            hand_on(RING - step).start()

    lax.fori_loop(0, steps + 6, pipeline, 0)

    for step in range(RING):
        hand_on(step).wait_recv()
    for b in range(RING):
        az(b).wait_recv()

    def put(which, k, out):
        return pltpu.make_async_copy(
            wfin.at[which, tile_rows(k)], out.at[tile_rows(k)], out_sem.at[which, k]
        )

    def weights(k, carry):
        here = tile_rows(k)
        dz(k).wait_recv()
        down = dot_tn(scl[:, tile_cols(mine, k)], hid[...]).astype(BF16).astype(F32)
        wfin[2, here, :] = (down + drecv[here, :].astype(F32)).astype(BF16)
        put(2, k, down_out).start()
        both = dot_tn(tok[:, tile_cols(mine, k)], act[...]) + dot_tn(
            tok_o[:, tile_cols(0, k)], act_o[...]
        )
        wfin[0, here, :] = both[:, :hl].astype(BF16)
        wfin[1, here, :] = both[:, hl:].astype(BF16)
        put(0, k, gate_out).start()
        put(1, k, up_out).start()
        return carry

    lax.fori_loop(0, tiles, weights, 0)

    swap_out = swap_matrix(group, slots, nodes)

    def put_rows(q):
        cols = pl.ds(pl.multiple_of(q * chunk, chunk), chunk)
        return pltpu.make_async_copy(dfin.at[q], dtok_out.at[:, cols], out_sem.at[3, q])

    def collect(q, carry):
        to_nodes(q).wait_recv()
        got = arecv[q].astype(F32).reshape(group, chunk).astype(BF16)
        dfin[q] = jnp.dot(swap_out, got, preferred_element_type=F32).astype(BF16)
        put_rows(q).start()
        return carry

    lax.fori_loop(0, steps, collect, 0)

    for b in range(RING):
        tz(b).wait_send()
        az(b).wait_send()
    for step in range(1, RING):
        for p in range(RING):
            spread(step, p).wait_send()
    for step in range(RING):
        hand_on(step).wait_send()

    def drain(q, carry):
        to_mate(q).wait_send()
        for way in range(2):
            opposite(q, way).wait_send()
            neighbour(q, way).wait_send()
        to_nodes(q).wait_send()
        put_rows(q).wait()
        return carry

    lax.fori_loop(0, steps, drain, 0)

    def drain_weights(k, carry):
        dz(k).wait_send()
        put(0, k, gate_out).wait()
        put(1, k, up_out).wait()
        put(2, k, down_out).wait()
        return carry

    lax.fori_loop(0, tiles, drain_weights, 0)


def copy_kernel(count, *refs):
    sources, results, held = refs[:count], refs[count : 2 * count], refs[2 * count : 3 * count]
    sems = refs[3 * count]
    reads, writes = [], []
    for i in range(count):
        part = sources[i].shape[0] // 2
        for h in range(2):
            span = pl.ds(h * part, part)
            reads.append(
                pltpu.make_async_copy(sources[i].at[span], held[i].at[span], sems.at[0, 2 * i + h])
            )
            writes.append(
                pltpu.make_async_copy(held[i].at[span], results[i].at[span], sems.at[1, 2 * i + h])
            )
    for read in reads:
        read.start()
    for read, write in zip(reads, writes):
        read.wait()
        write.start()
    for write in writes:
        write.wait()


def on_device(chunk, tile, tokens_in, grad_rows, combine_weights, live_counts, w_gate, w_up, w_down):
    slot_count, nodes, width = tokens_in.shape[2:]
    rows = slot_count * nodes
    hl = w_gate.shape[2]
    half = width // 2
    group = rows // (2 * RING)
    steps = width // chunk
    tiles = half // tile
    anywhere = pl.BlockSpec(memory_space=pl.ANY)
    dma = pltpu.SemaphoreType.DMA
    vmem = pltpu.VMEM
    weight_shape = jax.ShapeDtypeStruct((half, hl), BF16)
    held = pl.pallas_call(
        functools.partial(layer_kernel, nodes, chunk, tile),
        out_shape=(jax.ShapeDtypeStruct((group, width), BF16), weight_shape, weight_shape, weight_shape),
        in_specs=[anywhere, anywhere, pl.BlockSpec(memory_space=vmem),
                  pl.BlockSpec(memory_space=vmem), anywhere, anywhere, anywhere],
        out_specs=(anywhere, anywhere, anywhere, anywhere),
        scratch_shapes=[
            vmem((rows, width), BF16),
            vmem((rows, width), BF16),
            vmem((width, hl), BF16),
            vmem((width, hl), BF16),
            vmem((width, hl), BF16),
            vmem((rows, hl), BF16),
            vmem((rows, 2 * hl), BF16),
            vmem((rows, 2 * hl), BF16),
            vmem((rows, half), BF16),
            vmem((rows, 2 * hl), BF16),
            vmem((steps, rows // 2, chunk), BF16),
            vmem((steps, rows // 2, chunk), BF16),
            vmem((steps, rows // 2, chunk), BF16),
            vmem((steps, 2, group, chunk // 2), BF16),
            vmem((steps, 2, group, chunk), BF16),
            vmem((steps, nodes, group // nodes, chunk), BF16),
            vmem((steps, nodes, group // nodes, chunk), BF16),
            vmem((steps, group, chunk), BF16),
            vmem((half, hl), BF16),
            vmem((half, hl), BF16),
            vmem((3, half, hl), BF16),
            dma((3 + 2 * RING,)),
            dma((2, RING)),
            dma((2, RING)),
            dma((2, steps)),
            dma((2, RING, RING)),
            dma((2, RING)),
            dma((2, steps, 2)),
            dma((2, steps, 2)),
            dma((2, steps)),
            dma((2, tiles)),
            dma((4, max(tiles, steps))),
        ],
        compiler_params=pltpu.CompilerParams(
            collective_id=0, has_side_effects=True, vmem_limit_bytes=VMEM_LIMIT
        ),
        name="expert_backward",
    )(
        tokens_in[0, 0].reshape(rows, width),
        grad_rows[0, 0].reshape(rows, width),
        combine_weights[0, 0].T,
        live_counts[0],
        w_gate[0],
        w_up[0],
        w_down[0],
    )
    d_tokens, gate, up, down = pl.pallas_call(
        functools.partial(copy_kernel, len(held)),
        out_shape=tuple(jax.ShapeDtypeStruct(a.shape, a.dtype) for a in held),
        in_specs=[anywhere] * len(held),
        out_specs=tuple([anywhere] * len(held)),
        scratch_shapes=[vmem(a.shape, a.dtype) for a in held] + [dma((2, 2 * len(held)))],
        name="write_out",
    )(*held)
    return (
        d_tokens.reshape(1, 1, group // nodes, nodes, width),
        gate[None],
        up[None],
        down[None],
    )


VMEM_LIMIT = 62 * 1024 * 1024
CHUNK = 512
TILE = 256


def solution(mesh):
    return jax.shard_map(
        functools.partial(on_device, CHUNK, TILE),
        mesh=mesh,
        in_specs=(
            P("dp", "node", None, None, None),
            P("dp", "node", None, None, None),
            P("dp", "node", None, None),
            P("dp", "node", None),
            P("node", None, "local"),
            P("node", None, "local"),
            P("node", None, "local"),
        ),
        out_specs=(
            P("dp", "node", "local", None, None),
            P("node", "dp", "local"),
            P("node", "dp", "local"),
            P("node", "dp", "local"),
        ),
        check_vma=False,
    )
```

```python
import functools

import jax
import jax.numpy as jnp
from jax import lax
from jax.experimental import pallas as pl
from jax.experimental.pallas import tpu as pltpu
from jax.sharding import PartitionSpec as P

RING = 4
BF16 = jnp.bfloat16
F32 = jnp.float32


def dot_nt(a, b):
    return lax.dot_general(a, b, (((1,), (1,)), ((), ())), preferred_element_type=F32)


def dot_tn(a, b):
    return lax.dot_general(a, b, (((0,), (0,)), ((), ())), preferred_element_type=F32)


def swap_matrix(size, inner_in, inner_out):
    row = lax.broadcasted_iota(jnp.int32, (size, size), 0)
    col = lax.broadcasted_iota(jnp.int32, (size, size), 1)
    source = (row % inner_out) * inner_in + row // inner_out
    return (col == source).astype(BF16)


def layer_kernel(
    nodes, chunk, tile,
    tok_hbm, grd_hbm, weight_ref, count_ref, wg_hbm, wu_hbm, wd_hbm,
    dtok_out, gate_out, up_out, down_out,
    tok, scl, wg, wu, wd, hid, act, actp, tok_o, act_o,
    msend, mrecv, csum, orecv, nrecv, afin, arecv, dsend, drecv,
    load_sem, tz_sem, az_sem, m_sem, ag_sem, fw_sem, o_sem, n_sem, a_sem, dz_sem,
):
    rows, width = tok.shape
    hl = wg.shape[1]
    half = width // 2
    group = rows // (2 * RING)
    block = rows // RING
    slots = group // nodes
    piece = group // RING
    steps = width // chunk
    side = chunk // 2
    tiles = half // tile

    mine = lax.axis_index("dp")
    node = lax.axis_index("node")
    local = lax.axis_index("local")
    core = lax.rem(local, 2)
    place = lax.div(local, 2)
    other = 1 - mine
    mate = local + 1 - 2 * core

    def at_place(step):
        return lax.rem(place + step, RING)

    def peer(step):
        return at_place(step) * 2 + core

    def load(src, dst, index):
        return pltpu.make_async_copy(src, dst, load_sem.at[index])

    def block_rows(b):
        return pl.ds(pl.multiple_of(b * block, block), block)

    def tok_load(b):
        return load(tok_hbm.at[block_rows(b)], tok.at[block_rows(b)], 3 + b)

    def grd_load(b):
        return load(grd_hbm.at[block_rows(b)], scl.at[block_rows(b)], 3 + RING + b)

    load_wg = load(wg_hbm, wg, 0)
    load_wu = load(wu_hbm, wu, 1)
    load_wd = load(wd_hbm, wd, 2)
    load_wg.start()
    load_wu.start()
    tok_load(0).start()

    barrier = pltpu.get_barrier_semaphore()
    pl.semaphore_signal(barrier, inc=1, device_id={"dp": other})
    pl.semaphore_signal(barrier, inc=1, device_id={"local": mate})
    for step in range(1, RING):
        pl.semaphore_signal(barrier, inc=1, device_id={"local": peer(step)})

    def greet(i, carry):
        pl.semaphore_signal(barrier, inc=1, device_id={"node": lax.rem(node + i, nodes)})
        return carry

    lax.fori_loop(1, nodes, greet, 0)
    pl.semaphore_wait(barrier, 2 + RING - 1 + nodes - 1)

    def group_rows(l):
        return pl.ds(pl.multiple_of(l * group, group), group)

    def piece_rows(l, p):
        return pl.ds(pl.multiple_of(l * group + p * piece, piece), piece)

    def tz(p):
        return pltpu.make_async_remote_copy(
            tok_hbm.at[piece_rows(local, p), pl.ds(pl.multiple_of(other * half, 128), half)],
            tok_o.at[piece_rows(local, p)],
            tz_sem.at[0, p], tz_sem.at[1, p], device_id={"dp": other},
        )

    for p in range(RING):
        tz(p).start()
    grd_load(0).start()
    load_wd.start()
    tok_load(1).start()
    grd_load(1).start()

    def spread(step, p):
        return pltpu.make_async_remote_copy(
            tok_o.at[piece_rows(local, p)], tok_o.at[piece_rows(local, p)],
            ag_sem.at[0, step, p], ag_sem.at[1, step, p], device_id={"local": peer(step)},
        )

    def spread_piece(p):
        tz(p).wait_recv()
        for step in range(1, RING):
            spread(step, p).start()

    def az(b):
        return pltpu.make_async_remote_copy(
            act.at[block_rows(b)], act_o.at[block_rows(b)],
            az_sem.at[0, b], az_sem.at[1, b], device_id={"dp": other},
        )

    swap_in = swap_matrix(group, nodes, slots)

    eye = lax.broadcasted_iota(jnp.int32, (nodes, nodes), 0) == lax.broadcasted_iota(
        jnp.int32, (nodes, nodes), 1
    )
    counts = jnp.broadcast_to(count_ref[...].astype(F32), (nodes, nodes))
    counts = jnp.sum(jnp.where(eye, counts, 0.0), axis=1, keepdims=True)
    slot_total = weight_ref.shape[1]
    slot_at = lax.broadcasted_iota(jnp.int32, (nodes, slot_total), 1).astype(F32)
    live_weights = jnp.where(slot_at < counts, weight_ref[...], 0.0)
    row_weights = jnp.tile(live_weights, (block // nodes, 1))
    row_slot = lax.broadcasted_iota(jnp.int32, (block, slot_total), 0) // nodes
    slot_lane = lax.broadcasted_iota(jnp.int32, (block, slot_total), 1)

    load_wg.wait()
    load_wu.wait()

    def forward(b, carry):
        here = block_rows(b)
        tok_load(b).wait()
        grd_load(b).wait()

        @pl.when(b == 0)
        def _():
            load_wd.wait()

        @pl.when(b < RING - 2)
        def _():
            tok_load(b + 2).start()
            grd_load(b + 2).start()

        scale = jnp.sum(
            jnp.where(slot_lane == row_slot + b * (block // nodes), row_weights, 0.0),
            axis=1, keepdims=True,
        )
        rows_in = tok[here, :]
        gate = jnp.dot(rows_in, wg[...], preferred_element_type=F32)
        up = jnp.dot(rows_in, wu[...], preferred_element_type=F32)
        scaled = (scl[here, :].astype(F32) * scale).astype(BF16)
        scl[here, :] = scaled
        back = jnp.dot(scaled, wd[...], preferred_element_type=F32)
        sig = jax.nn.sigmoid(gate)
        silu = gate * sig
        hid[here, :] = (silu * up).astype(BF16)
        gate_grad = (back * up * sig * (1.0 + gate * (1.0 - sig))).astype(BF16)
        up_grad = (back * silu).astype(BF16)
        act[here, :hl] = gate_grad
        act[here, hl:] = up_grad
        az(b).start()
        for i in range(2):
            part = slice(i * group, (i + 1) * group)
            there = pl.ds(pl.multiple_of((i * RING + b) * group, group), group)
            actp[there, :hl] = jnp.dot(
                swap_in, gate_grad[part], preferred_element_type=F32
            ).astype(BF16)
            actp[there, hl:] = jnp.dot(
                swap_in, up_grad[part], preferred_element_type=F32
            ).astype(BF16)

        @pl.when(b >= 1)
        def _():
            spread_piece(b - 1)

        return carry

    lax.fori_loop(0, RING, forward, 0)

    def partial(which, q):
        cols = pl.ds(pl.multiple_of(q * chunk, chunk), chunk)
        here = pl.ds(pl.multiple_of(which * (rows // 2), rows // 2), rows // 2)
        return dot_nt(actp[here, :hl], wg[cols, :]) + dot_nt(actp[here, hl:], wu[cols, :])

    def to_mate(q):
        return pltpu.make_async_remote_copy(
            msend.at[q], mrecv.at[q], m_sem.at[0, q], m_sem.at[1, q], device_id={"local": mate}
        )

    def give(q):
        msend[q] = partial(1 - core, q).astype(BF16)
        to_mate(q).start()

    def hand_on(step):
        rows_of = group_rows(peer(step))
        return pltpu.make_async_remote_copy(
            tok_o.at[rows_of], tok_o.at[rows_of],
            fw_sem.at[0, step], fw_sem.at[1, step], device_id={"local": mate},
        )

    def part_rows(step):
        return pl.ds(pl.multiple_of(at_place(step) * group, group), group)

    def opposite(q, way):
        return pltpu.make_async_remote_copy(
            csum.at[q, part_rows(2), pl.ds(way * side, side)],
            orecv.at[q, way],
            o_sem.at[0, q, way], o_sem.at[1, q, way],
            device_id={"local": peer(1 if way == 0 else RING - 1)},
        )

    def neighbour(q, way):
        step = 1 if way == 0 else RING - 1
        return pltpu.make_async_remote_copy(
            csum.at[q, part_rows(step)],
            nrecv.at[q, way],
            n_sem.at[0, q, way], n_sem.at[1, q, way],
            device_id={"local": peer(step)},
        )

    def to_nodes(q):
        return pltpu.make_async_remote_copy(
            afin.at[q, pl.ds(0, nodes - 1)], arecv.at[q, pl.ds(0, nodes - 1)],
            a_sem.at[0, q], a_sem.at[1, q], device_id={"node": lax.rem(node + 1, nodes)},
        )

    def chip_sum(q):
        to_mate(q).wait_recv()
        total = partial(core, q) + mrecv[q].astype(F32)
        csum[q] = total.astype(BF16)
        opposite(q, 0).start()
        opposite(q, 1).start()

    def pass_on(q):
        for way in range(2):
            opposite(q, way).wait_recv()
            here = part_rows(1 if way == 0 else RING - 1)
            cols = slice(way * side, (way + 1) * side)
            csum[q, here, cols] = (
                csum[q, here, cols].astype(F32) + orecv[q, way].astype(F32)
            ).astype(BF16)
            neighbour(q, way).start()

    def finish(q):
        neighbour(q, 0).wait_recv()
        neighbour(q, 1).wait_recv()
        total = csum[q, part_rows(0)].astype(F32) + nrecv[q, 0].astype(F32) + nrecv[q, 1].astype(F32)
        afin[q] = total.reshape(nodes, slots, chunk).astype(BF16)
        arecv[q, node] = afin[q, node]

        def send(i, carry):
            to = lax.rem(node + i, nodes)
            pltpu.make_async_remote_copy(
                afin.at[q, to], arecv.at[q, node],
                a_sem.at[0, q], a_sem.at[1, q], device_id={"node": to},
            ).start()
            return carry

        lax.fori_loop(1, nodes, send, 0)

    def tile_cols(which, k):
        return pl.ds(pl.multiple_of(which * half + k * tile, 128), tile)

    def tile_rows(k):
        return pl.ds(pl.multiple_of(k * tile, tile), tile)

    def dz(k):
        return pltpu.make_async_remote_copy(
            dsend.at[tile_rows(k)], drecv.at[tile_rows(k)],
            dz_sem.at[0, k], dz_sem.at[1, k], device_id={"dp": other},
        )

    def down_other(k):
        dsend[tile_rows(k), :] = dot_tn(scl[:, tile_cols(other, k)], hid[...]).astype(BF16)
        dz(k).start()

    def pipeline(s, carry):
        @pl.when(s < steps)
        def _():
            give(s)

        @pl.when(s == 1)
        def _():
            spread_piece(RING - 1)
            hand_on(0).start()

        @pl.when(jnp.logical_and(s >= 2, s < steps + 2))
        def _():
            chip_sum(s - 2)

        for i in range(2):
            k = (s - 2) * 2 + i

            @pl.when(jnp.logical_and(k >= 0, k < tiles))
            def _():
                down_other(k)

        @pl.when(jnp.logical_and(s >= 4, s < steps + 4))
        def _():
            pass_on(s - 4)

        @pl.when(s == 6)
        def _():
            hand_on_arrivals()

        @pl.when(s >= 6)
        def _():
            finish(s - 6)

        return carry

    def hand_on_arrivals():
        for step in range(1, RING):
            for p in range(RING):
                rows_of = piece_rows(peer(RING - step), p)
                pltpu.make_async_remote_copy(
                    tok_o.at[rows_of], tok_o.at[rows_of],
                    ag_sem.at[0, step, p], ag_sem.at[1, step, p], device_id={"local": peer(step)},
                ).wait_recv()
            hand_on(RING - step).start()

    lax.fori_loop(0, steps + 6, pipeline, 0)

    for step in range(RING):
        hand_on(step).wait_recv()
    for b in range(RING):
        az(b).wait_recv()

    def weights(k, carry):
        here = tile_rows(k)
        dz(k).wait_recv()
        down = dot_tn(scl[:, tile_cols(mine, k)], hid[...]).astype(BF16).astype(F32)
        down_out[here, :] = (down + drecv[here, :].astype(F32)).astype(BF16)
        both = dot_tn(tok[:, tile_cols(mine, k)], act[...]) + dot_tn(
            tok_o[:, tile_cols(0, k)], act_o[...]
        )
        gate_out[here, :] = both[:, :hl].astype(BF16)
        up_out[here, :] = both[:, hl:].astype(BF16)
        return carry

    lax.fori_loop(0, tiles, weights, 0)

    swap_out = swap_matrix(group, slots, nodes)

    def collect(q, carry):
        to_nodes(q).wait_recv()
        got = arecv[q].astype(F32).reshape(group, chunk).astype(BF16)
        cols = pl.ds(pl.multiple_of(q * chunk, chunk), chunk)
        dtok_out[:, cols] = jnp.dot(swap_out, got, preferred_element_type=F32).astype(BF16)
        return carry

    lax.fori_loop(0, steps, collect, 0)

    for b in range(RING):
        tz(b).wait_send()
        az(b).wait_send()
    for step in range(1, RING):
        for p in range(RING):
            spread(step, p).wait_send()
    for step in range(RING):
        hand_on(step).wait_send()

    def drain(q, carry):
        to_mate(q).wait_send()
        for way in range(2):
            opposite(q, way).wait_send()
            neighbour(q, way).wait_send()
        to_nodes(q).wait_send()
        return carry

    lax.fori_loop(0, steps, drain, 0)

    def drain_weights(k, carry):
        dz(k).wait_send()
        return carry

    lax.fori_loop(0, tiles, drain_weights, 0)


def on_device(chunk, tile, tokens_in, grad_rows, combine_weights, live_counts, w_gate, w_up, w_down):
    slot_count, nodes, width = tokens_in.shape[2:]
    rows = slot_count * nodes
    hl = w_gate.shape[2]
    half = width // 2
    group = rows // (2 * RING)
    steps = width // chunk
    tiles = half // tile
    anywhere = pl.BlockSpec(memory_space=pl.ANY)
    dma = pltpu.SemaphoreType.DMA
    vmem = pltpu.VMEM
    weight_shape = vmem((half, hl), BF16)
    d_tokens, gate, up, down = pl.pallas_call(
        functools.partial(layer_kernel, nodes, chunk, tile),
        out_shape=(vmem((group, width), BF16), weight_shape, weight_shape, weight_shape),
        in_specs=[anywhere, anywhere, pl.BlockSpec(memory_space=vmem),
                  pl.BlockSpec(memory_space=vmem), anywhere, anywhere, anywhere],
        out_specs=tuple([pl.BlockSpec(memory_space=vmem)] * 4),
        scratch_shapes=[
            vmem((rows, width), BF16),
            vmem((rows, width), BF16),
            vmem((width, hl), BF16),
            vmem((width, hl), BF16),
            vmem((width, hl), BF16),
            vmem((rows, hl), BF16),
            vmem((rows, 2 * hl), BF16),
            vmem((rows, 2 * hl), BF16),
            vmem((rows, half), BF16),
            vmem((rows, 2 * hl), BF16),
            vmem((steps, rows // 2, chunk), BF16),
            vmem((steps, rows // 2, chunk), BF16),
            vmem((steps, rows // 2, chunk), BF16),
            vmem((steps, 2, group, chunk // 2), BF16),
            vmem((steps, 2, group, chunk), BF16),
            vmem((steps, nodes, group // nodes, chunk), BF16),
            vmem((steps, nodes, group // nodes, chunk), BF16),
            vmem((half, hl), BF16),
            vmem((half, hl), BF16),
            dma((3 + 2 * RING,)),
            dma((2, RING)),
            dma((2, RING)),
            dma((2, steps)),
            dma((2, RING, RING)),
            dma((2, RING)),
            dma((2, steps, 2)),
            dma((2, steps, 2)),
            dma((2, steps)),
            dma((2, tiles)),
        ],
        compiler_params=pltpu.CompilerParams(
            collective_id=0, has_side_effects=True, vmem_limit_bytes=VMEM_LIMIT
        ),
        name="expert_backward",
    )(
        tokens_in[0, 0].reshape(rows, width),
        grad_rows[0, 0].reshape(rows, width),
        combine_weights[0, 0].T,
        live_counts[0],
        w_gate[0],
        w_up[0],
        w_down[0],
    )
    return (
        d_tokens.reshape(1, 1, group // nodes, nodes, width),
        gate[None],
        up[None],
        down[None],
    )


VMEM_LIMIT = 56 * 1024 * 1024
CHUNK = 512
TILE = 256


def solution(mesh):
    return jax.shard_map(
        functools.partial(on_device, CHUNK, TILE),
        mesh=mesh,
        in_specs=(
            P("dp", "node", None, None, None),
            P("dp", "node", None, None, None),
            P("dp", "node", None, None),
            P("dp", "node", None),
            P("node", None, "local"),
            P("node", None, "local"),
            P("node", None, "local"),
        ),
        out_specs=(
            P("dp", "node", "local", None, None),
            P("node", "dp", "local"),
            P("node", "dp", "local"),
            P("node", "dp", "local"),
        ),
        check_vma=False,
    )
```

```python
import functools

import jax
import jax.numpy as jnp
from jax import lax
from jax.experimental import pallas as pl
from jax.experimental.pallas import tpu as pltpu
from jax.sharding import PartitionSpec as P

RING = 4
BF16 = jnp.bfloat16
F32 = jnp.float32


def dot_nt(a, b):
    return lax.dot_general(a, b, (((1,), (1,)), ((), ())), preferred_element_type=F32)


def dot_tn(a, b):
    return lax.dot_general(a, b, (((0,), (0,)), ((), ())), preferred_element_type=F32)


def swap_matrix(size, inner_in, inner_out):
    row = lax.broadcasted_iota(jnp.int32, (size, size), 0)
    col = lax.broadcasted_iota(jnp.int32, (size, size), 1)
    source = (row % inner_out) * inner_in + row // inner_out
    return (col == source).astype(BF16)


def layer_kernel(
    nodes, chunk, tile,
    tok_hbm, grd_hbm, weight_ref, count_ref, wg_hbm, wu_hbm, wd_hbm,
    dtok_out, gate_out, up_out, down_out,
    tok, scl, wg, wu, wd, hid, act, actp, tok_o, act_o,
    msend, mrecv, csum, orecv, nrecv, afin, arecv, dsend, drecv,
    load_sem, tz_sem, az_sem, m_sem, ag_sem, fw_sem, o_sem, n_sem, a_sem, dz_sem,
):
    rows, width = tok.shape
    hl = wg.shape[1]
    half = width // 2
    group = rows // (2 * RING)
    block = rows // RING
    slots = group // nodes
    piece = group // RING
    steps = width // chunk
    side = chunk // 2
    tiles = half // tile

    mine = lax.axis_index("dp")
    node = lax.axis_index("node")
    local = lax.axis_index("local")
    core = lax.rem(local, 2)
    place = lax.div(local, 2)
    other = 1 - mine
    mate = local + 1 - 2 * core

    def at_place(step):
        return lax.rem(place + step, RING)

    def peer(step):
        return at_place(step) * 2 + core

    def load(src, dst, index):
        return pltpu.make_async_copy(src, dst, load_sem.at[index])

    def block_rows(b):
        return pl.ds(pl.multiple_of(b * block, block), block)

    def tok_load(b):
        return load(tok_hbm.at[block_rows(b)], tok.at[block_rows(b)], 3 + b)

    def grd_load(b):
        return load(grd_hbm.at[block_rows(b)], scl.at[block_rows(b)], 3 + RING + b)

    load_wg = load(wg_hbm, wg, 0)
    load_wu = load(wu_hbm, wu, 1)
    load_wd = load(wd_hbm, wd, 2)
    load_wg.start()
    load_wu.start()
    tok_load(0).start()

    barrier = pltpu.get_barrier_semaphore()
    pl.semaphore_signal(barrier, inc=1, device_id={"dp": other})
    pl.semaphore_signal(barrier, inc=1, device_id={"local": mate})
    for step in range(1, RING):
        pl.semaphore_signal(barrier, inc=1, device_id={"local": peer(step)})

    def greet(i, carry):
        pl.semaphore_signal(barrier, inc=1, device_id={"node": lax.rem(node + i, nodes)})
        return carry

    lax.fori_loop(1, nodes, greet, 0)
    pl.semaphore_wait(barrier, 2 + RING - 1 + nodes - 1)

    def group_rows(l):
        return pl.ds(pl.multiple_of(l * group, group), group)

    def piece_rows(l, p):
        return pl.ds(pl.multiple_of(l * group + p * piece, piece), piece)

    def tz(p):
        return pltpu.make_async_remote_copy(
            tok_hbm.at[piece_rows(local, p), pl.ds(pl.multiple_of(other * half, 128), half)],
            tok_o.at[piece_rows(local, p)],
            tz_sem.at[0, p], tz_sem.at[1, p], device_id={"dp": other},
        )

    for p in range(RING):
        tz(p).start()
    grd_load(0).start()
    load_wd.start()
    tok_load(1).start()
    grd_load(1).start()

    def spread(step, p):
        return pltpu.make_async_remote_copy(
            tok_o.at[piece_rows(local, p)], tok_o.at[piece_rows(local, p)],
            ag_sem.at[0, step, p], ag_sem.at[1, step, p], device_id={"local": peer(step)},
        )

    def spread_piece(p):
        tz(p).wait_recv()
        for step in range(1, RING):
            spread(step, p).start()

    def az(b):
        return pltpu.make_async_remote_copy(
            act.at[block_rows(b)], act_o.at[block_rows(b)],
            az_sem.at[0, b], az_sem.at[1, b], device_id={"dp": other},
        )

    swap_in = swap_matrix(group, nodes, slots)

    eye = lax.broadcasted_iota(jnp.int32, (nodes, nodes), 0) == lax.broadcasted_iota(
        jnp.int32, (nodes, nodes), 1
    )
    counts = jnp.broadcast_to(count_ref[...].astype(F32), (nodes, nodes))
    counts = jnp.sum(jnp.where(eye, counts, 0.0), axis=1, keepdims=True)
    slot_total = weight_ref.shape[1]
    slot_at = lax.broadcasted_iota(jnp.int32, (nodes, slot_total), 1).astype(F32)
    live_weights = jnp.where(slot_at < counts, weight_ref[...], 0.0)
    row_weights = jnp.tile(live_weights, (block // nodes, 1))
    row_slot = lax.broadcasted_iota(jnp.int32, (block, slot_total), 0) // nodes
    slot_lane = lax.broadcasted_iota(jnp.int32, (block, slot_total), 1)

    load_wg.wait()
    load_wu.wait()

    def forward(b, carry):
        here = block_rows(b)
        tok_load(b).wait()
        grd_load(b).wait()

        @pl.when(b == 0)
        def _():
            load_wd.wait()

        @pl.when(b < RING - 2)
        def _():
            tok_load(b + 2).start()
            grd_load(b + 2).start()

        scale = jnp.sum(
            jnp.where(slot_lane == row_slot + b * (block // nodes), row_weights, 0.0),
            axis=1, keepdims=True,
        )
        rows_in = tok[here, :]
        gate = jnp.dot(rows_in, wg[...], preferred_element_type=F32)
        up = jnp.dot(rows_in, wu[...], preferred_element_type=F32)
        scaled = (scl[here, :].astype(F32) * scale).astype(BF16)
        scl[here, :] = scaled
        back = jnp.dot(scaled, wd[...], preferred_element_type=F32)
        sig = jax.nn.sigmoid(gate)
        silu = gate * sig
        hid[here, :] = (silu * up).astype(BF16)
        gate_grad = (back * up * sig * (1.0 + gate * (1.0 - sig))).astype(BF16)
        up_grad = (back * silu).astype(BF16)
        act[here, :hl] = gate_grad
        act[here, hl:] = up_grad
        az(b).start()
        for i in range(2):
            part = slice(i * group, (i + 1) * group)
            there = pl.ds(pl.multiple_of((i * RING + b) * group, group), group)
            actp[there, :hl] = jnp.dot(
                swap_in, gate_grad[part], preferred_element_type=F32
            ).astype(BF16)
            actp[there, hl:] = jnp.dot(
                swap_in, up_grad[part], preferred_element_type=F32
            ).astype(BF16)

        @pl.when(b >= 1)
        def _():
            spread_piece(b - 1)

        return carry

    lax.fori_loop(0, RING, forward, 0)

    def partial(which, q):
        cols = pl.ds(pl.multiple_of(q * chunk, chunk), chunk)
        here = pl.ds(pl.multiple_of(which * (rows // 2), rows // 2), rows // 2)
        return dot_nt(actp[here, :hl], wg[cols, :]) + dot_nt(actp[here, hl:], wu[cols, :])

    def to_mate(q):
        return pltpu.make_async_remote_copy(
            msend.at[q], mrecv.at[q], m_sem.at[0, q], m_sem.at[1, q], device_id={"local": mate}
        )

    def give(q):
        msend[q] = partial(1 - core, q).astype(BF16)
        to_mate(q).start()

    def hand_on(step):
        rows_of = group_rows(peer(step))
        return pltpu.make_async_remote_copy(
            tok_o.at[rows_of], tok_o.at[rows_of],
            fw_sem.at[0, step], fw_sem.at[1, step], device_id={"local": mate},
        )

    def part_rows(step):
        return pl.ds(pl.multiple_of(at_place(step) * group, group), group)

    def opposite(q, way):
        return pltpu.make_async_remote_copy(
            csum.at[q, part_rows(2), pl.ds(way * side, side)],
            orecv.at[q, way],
            o_sem.at[0, q, way], o_sem.at[1, q, way],
            device_id={"local": peer(1 if way == 0 else RING - 1)},
        )

    def neighbour(q, way):
        step = 1 if way == 0 else RING - 1
        return pltpu.make_async_remote_copy(
            csum.at[q, part_rows(step)],
            nrecv.at[q, way],
            n_sem.at[0, q, way], n_sem.at[1, q, way],
            device_id={"local": peer(step)},
        )

    def to_nodes(q):
        return pltpu.make_async_remote_copy(
            afin.at[q, pl.ds(0, nodes - 1)], arecv.at[q, pl.ds(0, nodes - 1)],
            a_sem.at[0, q], a_sem.at[1, q], device_id={"node": lax.rem(node + 1, nodes)},
        )

    def chip_sum(q):
        to_mate(q).wait_recv()
        total = partial(core, q) + mrecv[q].astype(F32)
        csum[q] = total.astype(BF16)
        opposite(q, 0).start()
        opposite(q, 1).start()

    def pass_on(q):
        for way in range(2):
            opposite(q, way).wait_recv()
            here = part_rows(1 if way == 0 else RING - 1)
            cols = slice(way * side, (way + 1) * side)
            csum[q, here, cols] = (
                csum[q, here, cols].astype(F32) + orecv[q, way].astype(F32)
            ).astype(BF16)
            neighbour(q, way).start()

    def finish(q):
        neighbour(q, 0).wait_recv()
        neighbour(q, 1).wait_recv()
        total = csum[q, part_rows(0)].astype(F32) + nrecv[q, 0].astype(F32) + nrecv[q, 1].astype(F32)
        afin[q] = total.reshape(nodes, slots, chunk).astype(BF16)
        arecv[q, node] = afin[q, node]

        def send(i, carry):
            to = lax.rem(node + i, nodes)
            pltpu.make_async_remote_copy(
                afin.at[q, to], arecv.at[q, node],
                a_sem.at[0, q], a_sem.at[1, q], device_id={"node": to},
            ).start()
            return carry

        lax.fori_loop(1, nodes, send, 0)

    def tile_cols(which, k):
        return pl.ds(pl.multiple_of(which * half + k * tile, 128), tile)

    def tile_rows(k):
        return pl.ds(pl.multiple_of(k * tile, tile), tile)

    def dz(k):
        return pltpu.make_async_remote_copy(
            dsend.at[tile_rows(k)], drecv.at[tile_rows(k)],
            dz_sem.at[0, k], dz_sem.at[1, k], device_id={"dp": other},
        )

    def down_other(k):
        dsend[tile_rows(k), :] = dot_tn(scl[:, tile_cols(other, k)], hid[...]).astype(BF16)
        dz(k).start()

    def pipeline(s, carry):
        @pl.when(s < steps)
        def _():
            give(s)

        @pl.when(s == 1)
        def _():
            spread_piece(RING - 1)
            hand_on(0).start()

        @pl.when(jnp.logical_and(s >= 2, s < steps + 2))
        def _():
            chip_sum(s - 2)

        for i in range(2):
            k = (s - 2) * 2 + i

            @pl.when(jnp.logical_and(k >= 0, k < tiles))
            def _():
                down_other(k)

        @pl.when(jnp.logical_and(s >= 4, s < steps + 4))
        def _():
            pass_on(s - 4)

        @pl.when(s == 6)
        def _():
            hand_on_arrivals()

        @pl.when(s >= 6)
        def _():
            finish(s - 6)

        return carry

    def hand_on_arrivals():
        for step in range(1, RING):
            for p in range(RING):
                rows_of = piece_rows(peer(RING - step), p)
                pltpu.make_async_remote_copy(
                    tok_o.at[rows_of], tok_o.at[rows_of],
                    ag_sem.at[0, step, p], ag_sem.at[1, step, p], device_id={"local": peer(step)},
                ).wait_recv()
            hand_on(RING - step).start()

    lax.fori_loop(0, steps + 6, pipeline, 0)

    for step in range(RING):
        hand_on(step).wait_recv()
    for b in range(RING):
        az(b).wait_recv()

    def weights(k, carry):
        here = tile_rows(k)
        dz(k).wait_recv()
        down = dot_tn(scl[:, tile_cols(mine, k)], hid[...]).astype(BF16).astype(F32)
        down_out[here, :] = (down + drecv[here, :].astype(F32)).astype(BF16)
        both = dot_tn(tok[:, tile_cols(mine, k)], act[...]) + dot_tn(
            tok_o[:, tile_cols(0, k)], act_o[...]
        )
        gate_out[here, :] = both[:, :hl].astype(BF16)
        up_out[here, :] = both[:, hl:].astype(BF16)
        return carry

    lax.fori_loop(0, tiles, weights, 0)

    swap_out = swap_matrix(group, slots, nodes)

    def collect(q, carry):
        to_nodes(q).wait_recv()
        got = arecv[q].astype(F32).reshape(group, chunk).astype(BF16)
        cols = pl.ds(pl.multiple_of(q * chunk, chunk), chunk)
        dtok_out[:, cols] = jnp.dot(swap_out, got, preferred_element_type=F32).astype(BF16)
        return carry

    lax.fori_loop(0, steps, collect, 0)

    for b in range(RING):
        tz(b).wait_send()
        az(b).wait_send()
    for step in range(1, RING):
        for p in range(RING):
            spread(step, p).wait_send()
    for step in range(RING):
        hand_on(step).wait_send()

    def drain(q, carry):
        to_mate(q).wait_send()
        for way in range(2):
            opposite(q, way).wait_send()
            neighbour(q, way).wait_send()
        to_nodes(q).wait_send()
        return carry

    lax.fori_loop(0, steps, drain, 0)

    def drain_weights(k, carry):
        dz(k).wait_send()
        return carry

    lax.fori_loop(0, tiles, drain_weights, 0)


def copy_kernel(count, *refs):
    sources, results, sems = refs[:count], refs[count : 2 * count], refs[2 * count]
    copies = []
    for i in range(count):
        part = sources[i].shape[0] // 2
        for h in range(2):
            span = pl.ds(h * part, part)
            copies.append(
                pltpu.make_async_copy(sources[i].at[span], results[i].at[span], sems.at[2 * i + h])
            )
    for copy in copies:
        copy.start()
    for copy in copies:
        copy.wait()


def on_device(chunk, tile, tokens_in, grad_rows, combine_weights, live_counts, w_gate, w_up, w_down):
    slot_count, nodes, width = tokens_in.shape[2:]
    rows = slot_count * nodes
    hl = w_gate.shape[2]
    half = width // 2
    group = rows // (2 * RING)
    steps = width // chunk
    tiles = half // tile
    anywhere = pl.BlockSpec(memory_space=pl.ANY)
    dma = pltpu.SemaphoreType.DMA
    vmem = pltpu.VMEM
    weight_shape = vmem((half, hl), BF16)
    held = pl.pallas_call(
        functools.partial(layer_kernel, nodes, chunk, tile),
        out_shape=(vmem((group, width), BF16), weight_shape, weight_shape, weight_shape),
        in_specs=[anywhere, anywhere, pl.BlockSpec(memory_space=vmem),
                  pl.BlockSpec(memory_space=vmem), anywhere, anywhere, anywhere],
        out_specs=tuple([pl.BlockSpec(memory_space=vmem)] * 4),
        scratch_shapes=[
            vmem((rows, width), BF16),
            vmem((rows, width), BF16),
            vmem((width, hl), BF16),
            vmem((width, hl), BF16),
            vmem((width, hl), BF16),
            vmem((rows, hl), BF16),
            vmem((rows, 2 * hl), BF16),
            vmem((rows, 2 * hl), BF16),
            vmem((rows, half), BF16),
            vmem((rows, 2 * hl), BF16),
            vmem((steps, rows // 2, chunk), BF16),
            vmem((steps, rows // 2, chunk), BF16),
            vmem((steps, rows // 2, chunk), BF16),
            vmem((steps, 2, group, chunk // 2), BF16),
            vmem((steps, 2, group, chunk), BF16),
            vmem((steps, nodes, group // nodes, chunk), BF16),
            vmem((steps, nodes, group // nodes, chunk), BF16),
            vmem((half, hl), BF16),
            vmem((half, hl), BF16),
            dma((3 + 2 * RING,)),
            dma((2, RING)),
            dma((2, RING)),
            dma((2, steps)),
            dma((2, RING, RING)),
            dma((2, RING)),
            dma((2, steps, 2)),
            dma((2, steps, 2)),
            dma((2, steps)),
            dma((2, tiles)),
        ],
        compiler_params=pltpu.CompilerParams(
            collective_id=0, has_side_effects=True, vmem_limit_bytes=VMEM_LIMIT
        ),
        name="expert_backward",
    )(
        tokens_in[0, 0].reshape(rows, width),
        grad_rows[0, 0].reshape(rows, width),
        combine_weights[0, 0].T,
        live_counts[0],
        w_gate[0],
        w_up[0],
        w_down[0],
    )
    held = [pltpu.with_memory_space_constraint(a, vmem) for a in held]
    d_tokens, gate, up, down = pl.pallas_call(
        functools.partial(copy_kernel, len(held)),
        out_shape=tuple(jax.ShapeDtypeStruct(a.shape, a.dtype) for a in held),
        in_specs=[pl.BlockSpec(memory_space=vmem)] * len(held),
        out_specs=tuple([anywhere] * len(held)),
        scratch_shapes=[dma((2 * len(held),))],
        compiler_params=pltpu.CompilerParams(vmem_limit_bytes=1024 * 1024),
        name="write_out",
    )(*held)
    return (
        d_tokens.reshape(1, 1, group // nodes, nodes, width),
        gate[None],
        up[None],
        down[None],
    )


VMEM_LIMIT = 56 * 1024 * 1024
CHUNK = 512
TILE = 256


def solution(mesh):
    return jax.shard_map(
        functools.partial(on_device, CHUNK, TILE),
        mesh=mesh,
        in_specs=(
            P("dp", "node", None, None, None),
            P("dp", "node", None, None, None),
            P("dp", "node", None, None),
            P("dp", "node", None),
            P("node", None, "local"),
            P("node", None, "local"),
            P("node", None, "local"),
        ),
        out_specs=(
            P("dp", "node", "local", None, None),
            P("node", "dp", "local"),
            P("node", "dp", "local"),
            P("node", "dp", "local"),
        ),
        check_vma=False,
    )
```

```python
import functools

import jax
import jax.numpy as jnp
from jax import lax
from jax.experimental import pallas as pl
from jax.experimental.pallas import tpu as pltpu
from jax.sharding import PartitionSpec as P

RING = 4
BF16 = jnp.bfloat16
F32 = jnp.float32


def dot_nt(a, b):
    return lax.dot_general(a, b, (((1,), (1,)), ((), ())), preferred_element_type=F32)


def dot_tn(a, b):
    return lax.dot_general(a, b, (((0,), (0,)), ((), ())), preferred_element_type=F32)


def swap_matrix(size, inner_in, inner_out):
    row = lax.broadcasted_iota(jnp.int32, (size, size), 0)
    col = lax.broadcasted_iota(jnp.int32, (size, size), 1)
    source = (row % inner_out) * inner_in + row // inner_out
    return (col == source).astype(BF16)


def layer_kernel(
    nodes, chunk, tile,
    tok_hbm, grd_hbm, weight_ref, count_ref, wg_hbm, wu_hbm, wd_hbm,
    dtok_out, gate_out, up_out, down_out,
    tok, scl, wg, wu, wd, hid, act, actp, tok_o, act_o,
    msend, mrecv, csum, orecv, nrecv, afin, arecv, dsend, drecv,
    load_sem, tz_sem, az_sem, m_sem, ag_sem, fw_sem, o_sem, n_sem, a_sem, dz_sem,
):
    rows, width = tok.shape
    hl = wg.shape[1]
    half = width // 2
    group = rows // (2 * RING)
    block = rows // RING
    slots = group // nodes
    piece = group // RING
    steps = width // chunk
    side = chunk // 2
    tiles = half // tile

    mine = lax.axis_index("dp")
    node = lax.axis_index("node")
    local = lax.axis_index("local")
    core = lax.rem(local, 2)
    place = lax.div(local, 2)
    other = 1 - mine
    mate = local + 1 - 2 * core

    def at_place(step):
        return lax.rem(place + step, RING)

    def peer(step):
        return at_place(step) * 2 + core

    def load(src, dst, index):
        return pltpu.make_async_copy(src, dst, load_sem.at[index])

    def block_rows(b):
        return pl.ds(pl.multiple_of(b * block, block), block)

    def tok_load(b):
        return load(tok_hbm.at[block_rows(b)], tok.at[block_rows(b)], 3 + b)

    def grd_load(b):
        return load(grd_hbm.at[block_rows(b)], scl.at[block_rows(b)], 3 + RING + b)

    load_wg = load(wg_hbm, wg, 0)
    load_wu = load(wu_hbm, wu, 1)
    load_wd = load(wd_hbm, wd, 2)

    barrier = pltpu.get_barrier_semaphore()
    pl.semaphore_signal(barrier, inc=1, device_id={"dp": other})
    pl.semaphore_signal(barrier, inc=1, device_id={"local": mate})
    for step in range(1, RING):
        pl.semaphore_signal(barrier, inc=1, device_id={"local": peer(step)})

    def greet(i, carry):
        pl.semaphore_signal(barrier, inc=1, device_id={"node": lax.rem(node + i, nodes)})
        return carry

    lax.fori_loop(1, nodes, greet, 0)
    load_wg.start()
    load_wu.start()
    tok_load(0).start()
    pl.semaphore_wait(barrier, 2 + RING - 1 + nodes - 1)

    def group_rows(l):
        return pl.ds(pl.multiple_of(l * group, group), group)

    def piece_rows(l, p):
        return pl.ds(pl.multiple_of(l * group + p * piece, piece), piece)

    def tz(p):
        return pltpu.make_async_remote_copy(
            tok_hbm.at[piece_rows(local, p), pl.ds(pl.multiple_of(other * half, 128), half)],
            tok_o.at[piece_rows(local, p)],
            tz_sem.at[0, p], tz_sem.at[1, p], device_id={"dp": other},
        )

    for p in range(RING):
        tz(p).start()
    grd_load(0).start()
    load_wd.start()
    tok_load(1).start()
    grd_load(1).start()

    def spread(step, p):
        return pltpu.make_async_remote_copy(
            tok_o.at[piece_rows(local, p)], tok_o.at[piece_rows(local, p)],
            ag_sem.at[0, step, p], ag_sem.at[1, step, p], device_id={"local": peer(step)},
        )

    def spread_piece(p):
        tz(p).wait_recv()
        for step in range(1, RING):
            spread(step, p).start()

    def az(b):
        return pltpu.make_async_remote_copy(
            act.at[block_rows(b)], act_o.at[block_rows(b)],
            az_sem.at[0, b], az_sem.at[1, b], device_id={"dp": other},
        )

    swap_in = swap_matrix(group, nodes, slots)

    eye = lax.broadcasted_iota(jnp.int32, (nodes, nodes), 0) == lax.broadcasted_iota(
        jnp.int32, (nodes, nodes), 1
    )
    counts = jnp.broadcast_to(count_ref[...].astype(F32), (nodes, nodes))
    counts = jnp.sum(jnp.where(eye, counts, 0.0), axis=1, keepdims=True)
    slot_total = weight_ref.shape[1]
    slot_at = lax.broadcasted_iota(jnp.int32, (nodes, slot_total), 1).astype(F32)
    live_weights = jnp.where(slot_at < counts, weight_ref[...], 0.0)
    row_weights = jnp.tile(live_weights, (block // nodes, 1))
    row_slot = lax.broadcasted_iota(jnp.int32, (block, slot_total), 0) // nodes
    slot_lane = lax.broadcasted_iota(jnp.int32, (block, slot_total), 1)

    load_wg.wait()
    load_wu.wait()

    def forward(b, carry):
        here = block_rows(b)
        tok_load(b).wait()
        grd_load(b).wait()

        @pl.when(b == 0)
        def _():
            load_wd.wait()

        @pl.when(b < RING - 2)
        def _():
            tok_load(b + 2).start()
            grd_load(b + 2).start()

        scale = jnp.sum(
            jnp.where(slot_lane == row_slot + b * (block // nodes), row_weights, 0.0),
            axis=1, keepdims=True,
        )
        rows_in = tok[here, :]
        gate = jnp.dot(rows_in, wg[...], preferred_element_type=F32)
        up = jnp.dot(rows_in, wu[...], preferred_element_type=F32)
        scaled = (scl[here, :].astype(F32) * scale).astype(BF16)
        scl[here, :] = scaled
        back = jnp.dot(scaled, wd[...], preferred_element_type=F32)
        sig = jax.nn.sigmoid(gate)
        silu = gate * sig
        hid[here, :] = (silu * up).astype(BF16)
        gate_grad = (back * up * sig * (1.0 + gate * (1.0 - sig))).astype(BF16)
        up_grad = (back * silu).astype(BF16)
        act[here, :hl] = gate_grad
        act[here, hl:] = up_grad
        az(b).start()
        for i in range(2):
            part = slice(i * group, (i + 1) * group)
            there = pl.ds(pl.multiple_of((i * RING + b) * group, group), group)
            actp[there, :hl] = jnp.dot(
                swap_in, gate_grad[part], preferred_element_type=F32
            ).astype(BF16)
            actp[there, hl:] = jnp.dot(
                swap_in, up_grad[part], preferred_element_type=F32
            ).astype(BF16)

        @pl.when(b >= 1)
        def _():
            spread_piece(b - 1)

        return carry

    lax.fori_loop(0, RING, forward, 0)

    def partial(which, q):
        cols = pl.ds(pl.multiple_of(q * chunk, chunk), chunk)
        here = pl.ds(pl.multiple_of(which * (rows // 2), rows // 2), rows // 2)
        return dot_nt(actp[here, :hl], wg[cols, :]) + dot_nt(actp[here, hl:], wu[cols, :])

    def to_mate(q):
        return pltpu.make_async_remote_copy(
            msend.at[q], mrecv.at[q], m_sem.at[0, q], m_sem.at[1, q], device_id={"local": mate}
        )

    def give(q):
        msend[q] = partial(1 - core, q).astype(BF16)
        to_mate(q).start()

    def hand_on(step):
        rows_of = group_rows(peer(step))
        return pltpu.make_async_remote_copy(
            tok_o.at[rows_of], tok_o.at[rows_of],
            fw_sem.at[0, step], fw_sem.at[1, step], device_id={"local": mate},
        )

    def part_rows(step):
        return pl.ds(pl.multiple_of(at_place(step) * group, group), group)

    def opposite(q, way):
        return pltpu.make_async_remote_copy(
            csum.at[q, part_rows(2), pl.ds(way * side, side)],
            orecv.at[q, way],
            o_sem.at[0, q, way], o_sem.at[1, q, way],
            device_id={"local": peer(1 if way == 0 else RING - 1)},
        )

    def neighbour(q, way):
        step = 1 if way == 0 else RING - 1
        return pltpu.make_async_remote_copy(
            csum.at[q, part_rows(step)],
            nrecv.at[q, way],
            n_sem.at[0, q, way], n_sem.at[1, q, way],
            device_id={"local": peer(step)},
        )

    def to_nodes(q):
        return pltpu.make_async_remote_copy(
            afin.at[q, pl.ds(0, nodes - 1)], arecv.at[q, pl.ds(0, nodes - 1)],
            a_sem.at[0, q], a_sem.at[1, q], device_id={"node": lax.rem(node + 1, nodes)},
        )

    def chip_sum(q):
        to_mate(q).wait_recv()
        total = partial(core, q) + mrecv[q].astype(F32)
        csum[q] = total.astype(BF16)
        opposite(q, 0).start()
        opposite(q, 1).start()

    def pass_on(q):
        for way in range(2):
            opposite(q, way).wait_recv()
            here = part_rows(1 if way == 0 else RING - 1)
            cols = slice(way * side, (way + 1) * side)
            csum[q, here, cols] = (
                csum[q, here, cols].astype(F32) + orecv[q, way].astype(F32)
            ).astype(BF16)
            neighbour(q, way).start()

    def finish(q):
        neighbour(q, 0).wait_recv()
        neighbour(q, 1).wait_recv()
        total = csum[q, part_rows(0)].astype(F32) + nrecv[q, 0].astype(F32) + nrecv[q, 1].astype(F32)
        afin[q] = total.reshape(nodes, slots, chunk).astype(BF16)
        arecv[q, node] = afin[q, node]

        def send(i, carry):
            to = lax.rem(node + i, nodes)
            pltpu.make_async_remote_copy(
                afin.at[q, to], arecv.at[q, node],
                a_sem.at[0, q], a_sem.at[1, q], device_id={"node": to},
            ).start()
            return carry

        lax.fori_loop(1, nodes, send, 0)

    def tile_cols(which, k):
        return pl.ds(pl.multiple_of(which * half + k * tile, 128), tile)

    def tile_rows(k):
        return pl.ds(pl.multiple_of(k * tile, tile), tile)

    def dz(k):
        return pltpu.make_async_remote_copy(
            dsend.at[tile_rows(k)], drecv.at[tile_rows(k)],
            dz_sem.at[0, k], dz_sem.at[1, k], device_id={"dp": other},
        )

    def down_other(k):
        dsend[tile_rows(k), :] = dot_tn(scl[:, tile_cols(other, k)], hid[...]).astype(BF16)
        dz(k).start()

    def pipeline(s, carry):
        @pl.when(s < steps)
        def _():
            give(s)

        @pl.when(s == 1)
        def _():
            spread_piece(RING - 1)
            hand_on(0).start()

        @pl.when(jnp.logical_and(s >= 2, s < steps + 2))
        def _():
            chip_sum(s - 2)

        for i in range(2):
            k = (s - 2) * 2 + i

            @pl.when(jnp.logical_and(k >= 0, k < tiles))
            def _():
                down_other(k)

        @pl.when(jnp.logical_and(s >= 4, s < steps + 4))
        def _():
            pass_on(s - 4)

        @pl.when(s == 6)
        def _():
            hand_on_arrivals()

        @pl.when(s >= 6)
        def _():
            finish(s - 6)

        return carry

    def hand_on_arrivals():
        for step in range(1, RING):
            for p in range(RING):
                rows_of = piece_rows(peer(RING - step), p)
                pltpu.make_async_remote_copy(
                    tok_o.at[rows_of], tok_o.at[rows_of],
                    ag_sem.at[0, step, p], ag_sem.at[1, step, p], device_id={"local": peer(step)},
                ).wait_recv()
            hand_on(RING - step).start()

    lax.fori_loop(0, steps + 6, pipeline, 0)

    for step in range(RING):
        hand_on(step).wait_recv()
    for b in range(RING):
        az(b).wait_recv()

    def weights(k, carry):
        here = tile_rows(k)
        dz(k).wait_recv()
        down = dot_tn(scl[:, tile_cols(mine, k)], hid[...]).astype(BF16).astype(F32)
        down_out[here, :] = (down + drecv[here, :].astype(F32)).astype(BF16)
        both = dot_tn(tok[:, tile_cols(mine, k)], act[...]) + dot_tn(
            tok_o[:, tile_cols(0, k)], act_o[...]
        )
        gate_out[here, :] = both[:, :hl].astype(BF16)
        up_out[here, :] = both[:, hl:].astype(BF16)
        return carry

    lax.fori_loop(0, tiles, weights, 0)

    for b in range(RING):
        tz(b).wait_send()
        az(b).wait_send()
    for step in range(1, RING):
        for p in range(RING):
            spread(step, p).wait_send()
    for step in range(RING):
        hand_on(step).wait_send()

    def drain(q, carry):
        to_mate(q).wait_send()
        for way in range(2):
            opposite(q, way).wait_send()
            neighbour(q, way).wait_send()
        return carry

    lax.fori_loop(0, steps, drain, 0)

    def drain_weights(k, carry):
        dz(k).wait_send()
        return carry

    lax.fori_loop(0, tiles, drain_weights, 0)

    swap_out = swap_matrix(group, slots, nodes)

    def collect(q, carry):
        to_nodes(q).wait_recv()
        got = arecv[q].astype(F32).reshape(group, chunk).astype(BF16)
        cols = pl.ds(pl.multiple_of(q * chunk, chunk), chunk)
        dtok_out[:, cols] = jnp.dot(swap_out, got, preferred_element_type=F32).astype(BF16)
        to_nodes(q).wait_send()
        return carry

    lax.fori_loop(0, steps, collect, 0)


def copy_kernel(count, *refs):
    sources, results, sems = refs[:count], refs[count : 2 * count], refs[2 * count]
    copies = []
    for i in range(count):
        part = sources[i].shape[0] // 2
        for h in range(2):
            span = pl.ds(h * part, part)
            copies.append(
                pltpu.make_async_copy(sources[i].at[span], results[i].at[span], sems.at[2 * i + h])
            )
    for copy in copies:
        copy.start()
    for copy in copies:
        copy.wait()


def on_device(chunk, tile, tokens_in, grad_rows, combine_weights, live_counts, w_gate, w_up, w_down):
    slot_count, nodes, width = tokens_in.shape[2:]
    rows = slot_count * nodes
    hl = w_gate.shape[2]
    half = width // 2
    group = rows // (2 * RING)
    steps = width // chunk
    tiles = half // tile
    anywhere = pl.BlockSpec(memory_space=pl.ANY)
    dma = pltpu.SemaphoreType.DMA
    vmem = pltpu.VMEM
    weight_shape = vmem((half, hl), BF16)
    held = pl.pallas_call(
        functools.partial(layer_kernel, nodes, chunk, tile),
        out_shape=(vmem((group, width), BF16), weight_shape, weight_shape, weight_shape),
        in_specs=[anywhere, anywhere, pl.BlockSpec(memory_space=vmem),
                  pl.BlockSpec(memory_space=vmem), anywhere, anywhere, anywhere],
        out_specs=tuple([pl.BlockSpec(memory_space=vmem)] * 4),
        scratch_shapes=[
            vmem((rows, width), BF16),
            vmem((rows, width), BF16),
            vmem((width, hl), BF16),
            vmem((width, hl), BF16),
            vmem((width, hl), BF16),
            vmem((rows, hl), BF16),
            vmem((rows, 2 * hl), BF16),
            vmem((rows, 2 * hl), BF16),
            vmem((rows, half), BF16),
            vmem((rows, 2 * hl), BF16),
            vmem((steps, rows // 2, chunk), BF16),
            vmem((steps, rows // 2, chunk), BF16),
            vmem((steps, rows // 2, chunk), BF16),
            vmem((steps, 2, group, chunk // 2), BF16),
            vmem((steps, 2, group, chunk), BF16),
            vmem((steps, nodes, group // nodes, chunk), BF16),
            vmem((steps, nodes, group // nodes, chunk), BF16),
            vmem((half, hl), BF16),
            vmem((half, hl), BF16),
            dma((3 + 2 * RING,)),
            dma((2, RING)),
            dma((2, RING)),
            dma((2, steps)),
            dma((2, RING, RING)),
            dma((2, RING)),
            dma((2, steps, 2)),
            dma((2, steps, 2)),
            dma((2, steps)),
            dma((2, tiles)),
        ],
        compiler_params=pltpu.CompilerParams(
            collective_id=0, has_side_effects=True, vmem_limit_bytes=VMEM_LIMIT
        ),
        name="expert_backward",
    )(
        tokens_in[0, 0].reshape(rows, width),
        grad_rows[0, 0].reshape(rows, width),
        combine_weights[0, 0].T,
        live_counts[0],
        w_gate[0],
        w_up[0],
        w_down[0],
    )
    held = [pltpu.with_memory_space_constraint(a, vmem) for a in held]
    d_tokens, gate, up, down = pl.pallas_call(
        functools.partial(copy_kernel, len(held)),
        out_shape=tuple(jax.ShapeDtypeStruct(a.shape, a.dtype) for a in held),
        in_specs=[pl.BlockSpec(memory_space=vmem)] * len(held),
        out_specs=tuple([anywhere] * len(held)),
        scratch_shapes=[dma((2 * len(held),))],
        compiler_params=pltpu.CompilerParams(vmem_limit_bytes=1024 * 1024),
        name="write_out",
    )(*held)
    return (
        d_tokens.reshape(1, 1, group // nodes, nodes, width),
        gate[None],
        up[None],
        down[None],
    )


VMEM_LIMIT = 56 * 1024 * 1024
CHUNK = 512
TILE = 256


def solution(mesh):
    return jax.shard_map(
        functools.partial(on_device, CHUNK, TILE),
        mesh=mesh,
        in_specs=(
            P("dp", "node", None, None, None),
            P("dp", "node", None, None, None),
            P("dp", "node", None, None),
            P("dp", "node", None),
            P("node", None, "local"),
            P("node", None, "local"),
            P("node", None, "local"),
        ),
        out_specs=(
            P("dp", "node", "local", None, None),
            P("node", "dp", "local"),
            P("node", "dp", "local"),
            P("node", "dp", "local"),
        ),
        check_vma=False,
    )
```

```python
import functools

import jax
import jax.numpy as jnp
from jax import lax
from jax.experimental import pallas as pl
from jax.experimental.pallas import tpu as pltpu
from jax.sharding import PartitionSpec as P

RING = 4
BF16 = jnp.bfloat16
F32 = jnp.float32


def dot_nt(a, b):
    return lax.dot_general(a, b, (((1,), (1,)), ((), ())), preferred_element_type=F32)


def dot_tn(a, b):
    return lax.dot_general(a, b, (((0,), (0,)), ((), ())), preferred_element_type=F32)


def swap_matrix(size, inner_in, inner_out):
    row = lax.broadcasted_iota(jnp.int32, (size, size), 0)
    col = lax.broadcasted_iota(jnp.int32, (size, size), 1)
    source = (row % inner_out) * inner_in + row // inner_out
    return (col == source).astype(BF16)


def layer_kernel(
    nodes, chunk, tile,
    tok_hbm, grd_hbm, weight_ref, count_ref, wg_hbm, wu_hbm, wd_hbm,
    dtok_out, gate_out, up_out, down_out,
    tok, scl, wg, wu, wd, hid, act, actp, tok_o, act_o,
    msend, mrecv, csum, orecv, nrecv, afin, arecv, dsend, drecv,
    load_sem, tz_sem, az_sem, m_sem, ag_sem, fw_sem, o_sem, n_sem, a_sem, dz_sem,
):
    rows, width = tok.shape
    hl = wg.shape[1]
    half = width // 2
    group = rows // (2 * RING)
    block = rows // RING
    slots = group // nodes
    piece = group // RING
    steps = width // chunk
    side = chunk // 2
    tiles = half // tile

    mine = lax.axis_index("dp")
    node = lax.axis_index("node")
    local = lax.axis_index("local")
    core = lax.rem(local, 2)
    place = lax.div(local, 2)
    other = 1 - mine
    mate = local + 1 - 2 * core

    def at_place(step):
        return lax.rem(place + step, RING)

    def peer(step):
        return at_place(step) * 2 + core

    def load(src, dst, index):
        return pltpu.make_async_copy(src, dst, load_sem.at[index])

    def block_rows(b):
        return pl.ds(pl.multiple_of(b * block, block), block)

    def tok_load(b):
        return load(tok_hbm.at[block_rows(b)], tok.at[block_rows(b)], 3 + b)

    def grd_load(b):
        return load(grd_hbm.at[block_rows(b)], scl.at[block_rows(b)], 3 + RING + b)

    load_wg = load(wg_hbm, wg, 0)
    load_wu = load(wu_hbm, wu, 1)
    load_wd = load(wd_hbm, wd, 2)
    load_wg.start()
    load_wu.start()
    tok_load(0).start()

    barrier = pltpu.get_barrier_semaphore()
    pl.semaphore_signal(barrier, inc=1, device_id={"dp": other})
    pl.semaphore_signal(barrier, inc=1, device_id={"local": mate})
    for step in range(1, RING):
        pl.semaphore_signal(barrier, inc=1, device_id={"local": peer(step)})

    def greet(i, carry):
        pl.semaphore_signal(barrier, inc=1, device_id={"node": lax.rem(node + i, nodes)})
        return carry

    lax.fori_loop(1, nodes, greet, 0)
    pl.semaphore_wait(barrier, 2 + RING - 1 + nodes - 1)

    def group_rows(l):
        return pl.ds(pl.multiple_of(l * group, group), group)

    def piece_rows(l, p):
        return pl.ds(pl.multiple_of(l * group + p * piece, piece), piece)

    def tz(p):
        return pltpu.make_async_remote_copy(
            tok_hbm.at[piece_rows(local, p), pl.ds(pl.multiple_of(other * half, 128), half)],
            tok_o.at[piece_rows(local, p)],
            tz_sem.at[0, p], tz_sem.at[1, p], device_id={"dp": other},
        )

    for p in range(RING):
        tz(p).start()
    grd_load(0).start()
    load_wd.start()

    def spread(step, p):
        return pltpu.make_async_remote_copy(
            tok_o.at[piece_rows(local, p)], tok_o.at[piece_rows(local, p)],
            ag_sem.at[0, step, p], ag_sem.at[1, step, p], device_id={"local": peer(step)},
        )

    def spread_piece(p):
        tz(p).wait_recv()
        for step in range(1, RING):
            spread(step, p).start()

    def az(b):
        return pltpu.make_async_remote_copy(
            act.at[block_rows(b)], act_o.at[block_rows(b)],
            az_sem.at[0, b], az_sem.at[1, b], device_id={"dp": other},
        )

    swap_in = swap_matrix(group, nodes, slots)

    eye = lax.broadcasted_iota(jnp.int32, (nodes, nodes), 0) == lax.broadcasted_iota(
        jnp.int32, (nodes, nodes), 1
    )
    counts = jnp.broadcast_to(count_ref[...].astype(F32), (nodes, nodes))
    counts = jnp.sum(jnp.where(eye, counts, 0.0), axis=1, keepdims=True)
    slot_total = weight_ref.shape[1]
    slot_at = lax.broadcasted_iota(jnp.int32, (nodes, slot_total), 1).astype(F32)
    live_weights = jnp.where(slot_at < counts, weight_ref[...], 0.0)
    row_weights = jnp.tile(live_weights, (block // nodes, 1))
    row_slot = lax.broadcasted_iota(jnp.int32, (block, slot_total), 0) // nodes
    slot_lane = lax.broadcasted_iota(jnp.int32, (block, slot_total), 1)

    load_wg.wait()
    load_wu.wait()

    def forward(b, carry):
        here = block_rows(b)
        tok_load(b).wait()
        grd_load(b).wait()

        @pl.when(b == 0)
        def _():
            load_wd.wait()

        @pl.when(b < RING - 1)
        def _():
            tok_load(b + 1).start()
            grd_load(b + 1).start()

        scale = jnp.sum(
            jnp.where(slot_lane == row_slot + b * (block // nodes), row_weights, 0.0),
            axis=1, keepdims=True,
        )
        rows_in = tok[here, :]
        gate = jnp.dot(rows_in, wg[...], preferred_element_type=F32)
        up = jnp.dot(rows_in, wu[...], preferred_element_type=F32)
        scaled = (scl[here, :].astype(F32) * scale).astype(BF16)
        scl[here, :] = scaled
        back = jnp.dot(scaled, wd[...], preferred_element_type=F32)
        sig = jax.nn.sigmoid(gate)
        silu = gate * sig
        hid[here, :] = (silu * up).astype(BF16)
        gate_grad = (back * up * sig * (1.0 + gate * (1.0 - sig))).astype(BF16)
        up_grad = (back * silu).astype(BF16)
        act[here, :hl] = gate_grad
        act[here, hl:] = up_grad
        az(b).start()
        for i in range(2):
            part = slice(i * group, (i + 1) * group)
            there = pl.ds(pl.multiple_of((i * RING + b) * group, group), group)
            actp[there, :hl] = jnp.dot(
                swap_in, gate_grad[part], preferred_element_type=F32
            ).astype(BF16)
            actp[there, hl:] = jnp.dot(
                swap_in, up_grad[part], preferred_element_type=F32
            ).astype(BF16)

        @pl.when(b >= 1)
        def _():
            spread_piece(b - 1)

        return carry

    lax.fori_loop(0, RING, forward, 0)

    def partial(which, q):
        cols = pl.ds(pl.multiple_of(q * chunk, chunk), chunk)
        here = pl.ds(pl.multiple_of(which * (rows // 2), rows // 2), rows // 2)
        return dot_nt(actp[here, :hl], wg[cols, :]) + dot_nt(actp[here, hl:], wu[cols, :])

    def to_mate(q):
        return pltpu.make_async_remote_copy(
            msend.at[q], mrecv.at[q], m_sem.at[0, q], m_sem.at[1, q], device_id={"local": mate}
        )

    def give(q):
        msend[q] = partial(1 - core, q).astype(BF16)
        to_mate(q).start()

    def hand_on(step):
        rows_of = group_rows(peer(step))
        return pltpu.make_async_remote_copy(
            tok_o.at[rows_of], tok_o.at[rows_of],
            fw_sem.at[0, step], fw_sem.at[1, step], device_id={"local": mate},
        )

    def part_rows(step):
        return pl.ds(pl.multiple_of(at_place(step) * group, group), group)

    def opposite(q, way):
        return pltpu.make_async_remote_copy(
            csum.at[q, part_rows(2), pl.ds(way * side, side)],
            orecv.at[q, way],
            o_sem.at[0, q, way], o_sem.at[1, q, way],
            device_id={"local": peer(1 if way == 0 else RING - 1)},
        )

    def neighbour(q, way):
        step = 1 if way == 0 else RING - 1
        return pltpu.make_async_remote_copy(
            csum.at[q, part_rows(step)],
            nrecv.at[q, way],
            n_sem.at[0, q, way], n_sem.at[1, q, way],
            device_id={"local": peer(step)},
        )

    def to_nodes(q):
        return pltpu.make_async_remote_copy(
            afin.at[q, pl.ds(0, nodes - 1)], arecv.at[q, pl.ds(0, nodes - 1)],
            a_sem.at[0, q], a_sem.at[1, q], device_id={"node": lax.rem(node + 1, nodes)},
        )

    def chip_sum(q):
        to_mate(q).wait_recv()
        total = partial(core, q) + mrecv[q].astype(F32)
        csum[q] = total.astype(BF16)
        opposite(q, 0).start()
        opposite(q, 1).start()

    def pass_on(q):
        for way in range(2):
            opposite(q, way).wait_recv()
            here = part_rows(1 if way == 0 else RING - 1)
            cols = slice(way * side, (way + 1) * side)
            csum[q, here, cols] = (
                csum[q, here, cols].astype(F32) + orecv[q, way].astype(F32)
            ).astype(BF16)
            neighbour(q, way).start()

    def finish(q):
        neighbour(q, 0).wait_recv()
        neighbour(q, 1).wait_recv()
        total = csum[q, part_rows(0)].astype(F32) + nrecv[q, 0].astype(F32) + nrecv[q, 1].astype(F32)
        afin[q] = total.reshape(nodes, slots, chunk).astype(BF16)
        arecv[q, node] = afin[q, node]

        def send(i, carry):
            to = lax.rem(node + i, nodes)
            pltpu.make_async_remote_copy(
                afin.at[q, to], arecv.at[q, node],
                a_sem.at[0, q], a_sem.at[1, q], device_id={"node": to},
            ).start()
            return carry

        lax.fori_loop(1, nodes, send, 0)

    def tile_cols(which, k):
        return pl.ds(pl.multiple_of(which * half + k * tile, 128), tile)

    def tile_rows(k):
        return pl.ds(pl.multiple_of(k * tile, tile), tile)

    def dz(k):
        return pltpu.make_async_remote_copy(
            dsend.at[tile_rows(k)], drecv.at[tile_rows(k)],
            dz_sem.at[0, k], dz_sem.at[1, k], device_id={"dp": other},
        )

    def down_other(k):
        dsend[tile_rows(k), :] = dot_tn(scl[:, tile_cols(other, k)], hid[...]).astype(BF16)
        dz(k).start()

    def pipeline(s, carry):
        @pl.when(s < steps)
        def _():
            give(s)

        @pl.when(s == 1)
        def _():
            spread_piece(RING - 1)
            hand_on(0).start()

        @pl.when(jnp.logical_and(s >= 2, s < steps + 2))
        def _():
            chip_sum(s - 2)

        for i in range(2):
            k = (s - 2) * 2 + i

            @pl.when(jnp.logical_and(k >= 0, k < tiles))
            def _():
                down_other(k)

        @pl.when(jnp.logical_and(s >= 4, s < steps + 4))
        def _():
            pass_on(s - 4)

        @pl.when(s == 6)
        def _():
            hand_on_arrivals()

        @pl.when(s >= 6)
        def _():
            finish(s - 6)

        return carry

    def hand_on_arrivals():
        for step in range(1, RING):
            for p in range(RING):
                rows_of = piece_rows(peer(RING - step), p)
                pltpu.make_async_remote_copy(
                    tok_o.at[rows_of], tok_o.at[rows_of],
                    ag_sem.at[0, step, p], ag_sem.at[1, step, p], device_id={"local": peer(step)},
                ).wait_recv()
            hand_on(RING - step).start()

    lax.fori_loop(0, steps + 6, pipeline, 0)

    for step in range(RING):
        hand_on(step).wait_recv()
    for b in range(RING):
        az(b).wait_recv()

    def weights(k, carry):
        here = tile_rows(k)
        dz(k).wait_recv()
        down = dot_tn(scl[:, tile_cols(mine, k)], hid[...]).astype(BF16).astype(F32)
        down_out[here, :] = (down + drecv[here, :].astype(F32)).astype(BF16)
        both = dot_tn(tok[:, tile_cols(mine, k)], act[...]) + dot_tn(
            tok_o[:, tile_cols(0, k)], act_o[...]
        )
        gate_out[here, :] = both[:, :hl].astype(BF16)
        up_out[here, :] = both[:, hl:].astype(BF16)
        return carry

    lax.fori_loop(0, tiles, weights, 0)

    swap_out = swap_matrix(group, slots, nodes)

    def collect(q, carry):
        to_nodes(q).wait_recv()
        got = arecv[q].astype(F32).reshape(group, chunk).astype(BF16)
        cols = pl.ds(pl.multiple_of(q * chunk, chunk), chunk)
        dtok_out[:, cols] = jnp.dot(swap_out, got, preferred_element_type=F32).astype(BF16)
        return carry

    lax.fori_loop(0, steps, collect, 0)

    for b in range(RING):
        tz(b).wait_send()
        az(b).wait_send()
    for step in range(1, RING):
        for p in range(RING):
            spread(step, p).wait_send()
    for step in range(RING):
        hand_on(step).wait_send()

    def drain(q, carry):
        to_mate(q).wait_send()
        for way in range(2):
            opposite(q, way).wait_send()
            neighbour(q, way).wait_send()
        to_nodes(q).wait_send()
        return carry

    lax.fori_loop(0, steps, drain, 0)

    def drain_weights(k, carry):
        dz(k).wait_send()
        return carry

    lax.fori_loop(0, tiles, drain_weights, 0)


def copy_kernel(count, *refs):
    sources, results, sems = refs[:count], refs[count : 2 * count], refs[2 * count]
    copies = []
    for i in range(count):
        part = sources[i].shape[0] // 2
        for h in range(2):
            span = pl.ds(h * part, part)
            copies.append(
                pltpu.make_async_copy(sources[i].at[span], results[i].at[span], sems.at[2 * i + h])
            )
    for copy in copies:
        copy.start()
    for copy in copies:
        copy.wait()


def on_device(chunk, tile, tokens_in, grad_rows, combine_weights, live_counts, w_gate, w_up, w_down):
    slot_count, nodes, width = tokens_in.shape[2:]
    rows = slot_count * nodes
    hl = w_gate.shape[2]
    half = width // 2
    group = rows // (2 * RING)
    steps = width // chunk
    tiles = half // tile
    anywhere = pl.BlockSpec(memory_space=pl.ANY)
    dma = pltpu.SemaphoreType.DMA
    vmem = pltpu.VMEM
    weight_shape = vmem((half, hl), BF16)
    held = pl.pallas_call(
        functools.partial(layer_kernel, nodes, chunk, tile),
        out_shape=(vmem((group, width), BF16), weight_shape, weight_shape, weight_shape),
        in_specs=[anywhere, anywhere, pl.BlockSpec(memory_space=vmem),
                  pl.BlockSpec(memory_space=vmem), anywhere, anywhere, anywhere],
        out_specs=tuple([pl.BlockSpec(memory_space=vmem)] * 4),
        scratch_shapes=[
            vmem((rows, width), BF16),
            vmem((rows, width), BF16),
            vmem((width, hl), BF16),
            vmem((width, hl), BF16),
            vmem((width, hl), BF16),
            vmem((rows, hl), BF16),
            vmem((rows, 2 * hl), BF16),
            vmem((rows, 2 * hl), BF16),
            vmem((rows, half), BF16),
            vmem((rows, 2 * hl), BF16),
            vmem((steps, rows // 2, chunk), BF16),
            vmem((steps, rows // 2, chunk), BF16),
            vmem((steps, rows // 2, chunk), BF16),
            vmem((steps, 2, group, chunk // 2), BF16),
            vmem((steps, 2, group, chunk), BF16),
            vmem((steps, nodes, group // nodes, chunk), BF16),
            vmem((steps, nodes, group // nodes, chunk), BF16),
            vmem((half, hl), BF16),
            vmem((half, hl), BF16),
            dma((3 + 2 * RING,)),
            dma((2, RING)),
            dma((2, RING)),
            dma((2, steps)),
            dma((2, RING, RING)),
            dma((2, RING)),
            dma((2, steps, 2)),
            dma((2, steps, 2)),
            dma((2, steps)),
            dma((2, tiles)),
        ],
        compiler_params=pltpu.CompilerParams(
            collective_id=0, has_side_effects=True, vmem_limit_bytes=VMEM_LIMIT
        ),
        name="expert_backward",
    )(
        tokens_in[0, 0].reshape(rows, width),
        grad_rows[0, 0].reshape(rows, width),
        combine_weights[0, 0].T,
        live_counts[0],
        w_gate[0],
        w_up[0],
        w_down[0],
    )
    held = [pltpu.with_memory_space_constraint(a, vmem) for a in held]
    d_tokens, gate, up, down = pl.pallas_call(
        functools.partial(copy_kernel, len(held)),
        out_shape=tuple(jax.ShapeDtypeStruct(a.shape, a.dtype) for a in held),
        in_specs=[pl.BlockSpec(memory_space=vmem)] * len(held),
        out_specs=tuple([anywhere] * len(held)),
        scratch_shapes=[dma((2 * len(held),))],
        compiler_params=pltpu.CompilerParams(vmem_limit_bytes=1024 * 1024),
        name="write_out",
    )(*held)
    return (
        d_tokens.reshape(1, 1, group // nodes, nodes, width),
        gate[None],
        up[None],
        down[None],
    )


VMEM_LIMIT = 56 * 1024 * 1024
CHUNK = 512
TILE = 256


def solution(mesh):
    return jax.shard_map(
        functools.partial(on_device, CHUNK, TILE),
        mesh=mesh,
        in_specs=(
            P("dp", "node", None, None, None),
            P("dp", "node", None, None, None),
            P("dp", "node", None, None),
            P("dp", "node", None),
            P("node", None, "local"),
            P("node", None, "local"),
            P("node", None, "local"),
        ),
        out_specs=(
            P("dp", "node", "local", None, None),
            P("node", "dp", "local"),
            P("node", "dp", "local"),
            P("node", "dp", "local"),
        ),
        check_vma=False,
    )
```
